256 devices in a mesh: ctx: 8 (over z_lo, y), exp: 32 (over z_hi, x, core).
Axes of the slice: x: 4, y: 4, z: 8 (z_hi: 4, z_lo: 2; z = z_hi * 2 + z_lo), core: 2. Of those that a mesh axis runs over, the one named last changes fastest.
Arguments:
- tokens: bfloat16 [32, 1024, 2048], P('exp', 'ctx'), may hold values from -6 to 6
- queries: bfloat16 [32, 1024, 1024], P('exp', 'ctx'), may hold values from -60 to 60
- keys: bfloat16 [32, 1024, 1024], P('exp', 'ctx'), may hold values from -4 to 4
- values: bfloat16 [32, 1024, 1024], P('exp', 'ctx'), may hold values from -12 to 12
- out_proj: bfloat16 [1024, 2048], replicated, may hold values from -0.1875 to 0.1875
- mod_scale: float32 [32, 2048], P('exp'), may hold values from -2.5 to 2.5
- mod_shift: float32 [32, 2048], P('exp'), may hold values from -2.5 to 2.5
- expert_ids: int32 [32, 1024, 2], P('exp', 'ctx'), may hold values from 0 to 63, all different within a row; in each aligned block of 128 rows (0 to 127, 128 to 255, ..., all dimensions but the last counted through in order) at most 6 rows name the same one
- gates: float32 [32, 1024, 2], P('exp', 'ctx'), may hold values from 0.2 to 1
- w_gate: bfloat16 [65536, 2048], P(('ctx', 'exp')), may hold values from -0.125 to 0.125
- w_up: bfloat16 [65536, 2048], P(('ctx', 'exp')), may hold values from -0.125 to 0.125
- w_down: bfloat16 [65536, 2048], P(('ctx', 'exp')), may hold values from -0.1875 to 0.1875
- out_grad: bfloat16 [32, 1024, 2048], P('exp', 'ctx'), may hold values from -0.1875 to 0.1875
Outputs:
- layer_out: bfloat16 [32, 1024, 2048], P('exp', 'ctx')
- grad_gate: bfloat16 [65536, 2048], P(('ctx', 'exp'))
- grad_up: bfloat16 [65536, 2048], P(('ctx', 'exp'))
- grad_down: bfloat16 [65536, 2048], P(('ctx', 'exp'))
The draws below stay inside these ranges and needn't reach their ends.
Inputs may be any that keep to these rules, and one draw needn't show every extreme that they name: `expert_ids`: the two ids of a token differ. Among the 128 tokens of one device no expert is named more than 6 times, and in some device some expert exactly 6 times.
All inputs are finite; a program needn't handle non-finite values.
Results may differ from the reference program's by a relative error of at most 0.0075.
Values may be sent and summed in bfloat16 or wider, within the bound.
A program may use at most 128 MiB of HBM per device.

```python
import math
import jax
import jax.numpy as jnp
import numpy as np
from jax import lax

D = 2048
F = 1024
HEADS = 8
HD = 128
SHARDS = 4
TOK_DEV = 128
SEQS = 32
LENGTH = 1024
EXPERTS = 64
CAP = 6
FS = 256
N_CTX = 8


def attention_pair(key):
    shape = (SEQS, LENGTH, HEADS * HD)
    key_base = jax.random.fold_in(key, 101)
    query_base = jax.random.fold_in(key, 202)
    key_draw = jax.random.truncated_normal(key_base, -4.0, 4.0, shape, jnp.float32)
    query_draw = jax.random.truncated_normal(query_base, -4.0, 4.0, shape, jnp.float32)
    return (query_draw, key_draw)


def draw_queries(key, part):
    return attention_pair(key)[0].astype(jnp.bfloat16)


def draw_keys(key, part):
    return attention_pair(key)[1].astype(jnp.bfloat16)


def levels(key, extent, cuts, smallest, top_value):
    gain, own = 1.0, jax.random.fold_in(key, 6)
    for dim, shards_of in cuts:
        steps = jnp.exp(jax.random.uniform(jax.random.fold_in(own, dim), (shards_of,), jnp.float32, smallest / len(cuts), top_value / len(cuts)))
        gain = gain * jnp.repeat(steps, extent[dim] // shards_of).reshape([-1 if axis == dim else 1 for axis in range(len(extent))])
    return gain


def routed_block(key, own, number, rows, number_of, top, most, slope):
    order = jax.random.permutation(key, number_of)
    heavy_load, common = load_shares(number_of, rows * top, most, slope, True), load_shares(number_of, rows * top, most, slope, False)
    places = jnp.arange(number_of)

    def named(lengths, rotation):
        used = int((lengths > 0).sum())
        fixed = max(1, used // 4)
        shifted = fixed + (places - fixed + rotation * (used - fixed)) % max(1, number_of - fixed)
        return jnp.zeros((number_of,), jnp.int32).at[order[jnp.where(places < fixed, places, shifted)]].set(jnp.asarray(lengths, jnp.int32))

    lengths = jnp.where(number % 4 == 0, named(heavy_load, number // 4), named(common, number - number // 4 - 1))
    mixed = jax.random.permutation(jax.random.fold_in(own, 3), number_of)
    giver, receiver = mixed[0:number_of // 2 * 2:2], mixed[1:number_of // 2 * 2:2]
    slack = jnp.minimum(lengths[giver] - 1, most - lengths[receiver]) // 2
    slack = jnp.where((giver == order[0]) | (receiver == order[0]) | (lengths[receiver] == 0), 0, jnp.maximum(slack, 0))
    shifted = jax.random.randint(jax.random.fold_in(own, 4), (number_of // 2,), 0, 1 << 20) % (slack + 1)
    lengths = lengths.at[giver].add(-shifted).at[receiver].add(shifted)
    members = jnp.searchsorted(jnp.cumsum(lengths), jnp.arange(rows * top), side="right").astype(jnp.int32)
    grid = members.reshape(top, rows).T
    grid = grid[jax.random.permutation(jax.random.fold_in(own, 1), rows)]
    rotation = jax.random.randint(jax.random.fold_in(own, 2), (rows, 1), 0, top)
    return jnp.take_along_axis(grid, (jnp.arange(top)[None, :] + rotation) % top, axis=1)


def load_shares(count, total, bound, slope, full):
    loads = [(1 << 20) // math.isqrt(rank ** slope) + 1 for rank in range(1, count + 1)]
    largest = bound if full else min(bound, max(-(-total // count), total * loads[0] // sum(loads)))
    least = 1 if total - largest >= count - 1 else 0
    holding, surplus = [largest] + [least] * (count - 1), total - largest - least * (count - 1)
    while surplus > 0:
        candidates = [i for i in range(1, count) if holding[i] < largest] or [i for i in range(1, count) if holding[i] < bound]
        pool, remaining = sum([loads[i] for i in candidates]), surplus
        for i in candidates:
            more = min(bound - holding[i], max(1, remaining * loads[i] // pool), surplus)
            holding[i] = holding[i] + more
            surplus = surplus - more
    return np.array(holding)


def gaussian(stream_key, extent, deviation, most, split=(), held_as=jnp.bfloat16):
    level = levels(stream_key, extent, split, -0.22, 0.18) if split else 1.0
    values = jax.random.normal(stream_key, extent, jnp.float32) * deviation * level
    return jnp.minimum(jnp.maximum(values, -most), most).astype(held_as)


def setup_inputs(seed: int = 0) -> dict:
    key_of = jax.random.split(jax.random.key(seed), 14)
    tokens = gaussian(key_of[0], (SEQS, LENGTH, D), 1.0, 6.0, ((0, 32), (1, 8)))
    queries = draw_queries(jax.random.fold_in(key_of[13], 71), 0)
    keys = draw_keys(jax.random.fold_in(key_of[13], 71), 0)
    values = gaussian(key_of[3], (SEQS, LENGTH, HEADS * HD), 3.0, 12.0, ((0, 32), (1, 8)))
    out_proj = gaussian(key_of[4], (HEADS * HD, D), (HEADS * HD) ** -0.5, 0.1875)
    mod_scale = gaussian(key_of[5], (SEQS, D), 0.3, 2.5, ((0, 32),), jnp.float32)
    mod_shift = gaussian(key_of[6], (SEQS, D), 0.5, 2.5, ((0, 32),), jnp.float32)
    expert_ids_keys = jax.random.split(jax.random.fold_in(key_of[7], 1), SEQS * LENGTH // TOK_DEV)
    expert_ids_turns = jax.random.permutation(jax.random.fold_in(key_of[7], 3), SEQS * LENGTH // TOK_DEV)
    expert_ids = jax.vmap(lambda own, number: routed_block(jax.random.fold_in(key_of[7], 2), own, number, TOK_DEV, EXPERTS, 2, CAP, 2))(expert_ids_keys, expert_ids_turns).reshape((SEQS, LENGTH, 2))
    gates = jnp.clip(jnp.exp(math.log(1.0) - 1.609438 * jax.random.uniform(key_of[8], (SEQS, LENGTH, 2), jnp.float32) ** levels(key_of[8], (SEQS, LENGTH, 2), ((0, 32), (1, 8)), -0.2, 0.2)), 0.2, 1.0)
    w_gate = gaussian(key_of[9], (EXPERTS * F, D), D ** -0.5, 0.125, ((0, 256),))
    w_up = gaussian(key_of[10], (EXPERTS * F, D), D ** -0.5, 0.125, ((0, 256),))
    w_down = gaussian(key_of[11], (EXPERTS * F, D), F ** -0.5, 0.1875, ((0, 256),))
    out_grad = gaussian(key_of[12], (SEQS, LENGTH, D), 0.03, 0.1875, ((0, 32), (1, 8)))
    return {"tokens": tokens, "queries": queries, "keys": keys, "values": values, "out_proj": out_proj, "mod_scale": mod_scale, "mod_shift": mod_shift, "expert_ids": expert_ids, "gates": gates, "w_gate": w_gate, "w_up": w_up, "w_down": w_down, "out_grad": out_grad}


def attend(bundle):
    query_seq, key_seq, value_seq = bundle
    length = query_seq.shape[0]
    query_heads = query_seq.astype(jnp.float32).reshape(length, HEADS, HD)
    key_heads = key_seq.astype(jnp.float32).reshape(length, HEADS, HD)
    value_heads = value_seq.astype(jnp.float32).reshape(length, HEADS, HD)
    scores = jnp.einsum('qhd,khd->hqk', query_heads, key_heads) * HD ** (-0.5)
    row_top = lax.optimization_barrier(jnp.max(scores, axis=-1, keepdims=True))
    exponent = jnp.exp(scores - row_top)
    denominator = lax.optimization_barrier(jnp.sum(exponent, axis=-1))
    rounded = lax.optimization_barrier(exponent.astype(jnp.bfloat16))
    mixed_heads = jnp.einsum('hqk,khd->hqd', rounded.astype(jnp.float32), value_heads) / denominator[..., None]
    return jnp.transpose(mixed_heads, (1, 0, 2)).reshape(length, HEADS * HD).astype(jnp.bfloat16)

def by_device(source_array):
    trailing = source_array.shape[2:]
    shaped = source_array.reshape((SEQS, N_CTX, TOK_DEV) + trailing)
    return jnp.swapaxes(shaped, 0, 1).reshape((N_CTX * SEQS, TOK_DEV) + trailing)

def expert_pass(bundle):
    expert_rows, row_grads, weight_gate, weight_up, weight_down = bundle
    gate_pre = jnp.dot(expert_rows, weight_gate.T, preferred_element_type=jnp.float32)
    up_pre = jnp.dot(expert_rows, weight_up.T, preferred_element_type=jnp.float32)
    sigmoid_gate = jax.nn.sigmoid(gate_pre)
    activation = gate_pre * sigmoid_gate
    hidden = (activation * up_pre).astype(jnp.bfloat16)
    expert_out = jnp.zeros((expert_rows.shape[0], D), jnp.float32)
    for shard_index in range(SHARDS):
        lower = shard_index * FS
        piece_out = jnp.dot(hidden[:, lower:lower + FS], weight_down[lower:lower + FS], preferred_element_type=jnp.float32)
        piece_out = lax.optimization_barrier(piece_out.astype(jnp.bfloat16))
        expert_out = expert_out + piece_out.astype(jnp.float32)
    hidden_grad = jnp.dot(row_grads, weight_down.T, preferred_element_type=jnp.float32)
    gate_cot = (hidden_grad * up_pre * sigmoid_gate * (1.0 + gate_pre * (1.0 - sigmoid_gate))).astype(jnp.bfloat16)
    up_cot = (hidden_grad * activation).astype(jnp.bfloat16)
    grad_down = jnp.dot(hidden.T, row_grads, preferred_element_type=jnp.float32).astype(jnp.bfloat16)
    grad_gate = jnp.dot(gate_cot.T, expert_rows, preferred_element_type=jnp.float32).astype(jnp.bfloat16)
    grad_up = jnp.dot(up_cot.T, expert_rows, preferred_element_type=jnp.float32).astype(jnp.bfloat16)
    return (expert_out, grad_gate, grad_up, grad_down)

def reference(tokens, queries, keys, values, out_proj, mod_scale, mod_shift, expert_ids, gates, w_gate, w_up, w_down, out_grad):
    attended = lax.map(attend, (queries, keys, values))
    projected = jnp.dot(attended.reshape(SEQS * LENGTH, HEADS * HD), out_proj, preferred_element_type=jnp.float32)
    mixed = tokens.astype(jnp.float32) + projected.reshape(SEQS, LENGTH, D)
    mean_square = lax.optimization_barrier(jnp.mean(mixed * mixed, axis=-1, keepdims=True))
    normed = (mixed * lax.rsqrt(mean_square + 1e-06) * (1.0 + mod_scale[:, None, :]) + mod_shift[:, None, :]).astype(jnp.bfloat16)
    devices = N_CTX * SEQS
    chosen = by_device(expert_ids).reshape(devices, 2 * TOK_DEV)
    one_hot = (chosen[:, :, None] == jnp.arange(EXPERTS, dtype=jnp.int32)[None, None, :]).astype(jnp.int32)
    before = jnp.cumsum(one_hot, axis=1) - one_hot
    slot_index = lax.optimization_barrier(jnp.sum(one_hot * before, axis=2))
    sources = jnp.broadcast_to(jnp.arange(devices, dtype=jnp.int32)[:, None], chosen.shape)
    flat_pos = ((chosen * devices + sources) * CAP + slot_index).reshape(-1).astype(jnp.int32)
    normed_rows = jnp.repeat(by_device(normed).reshape(devices * TOK_DEV, D), 2, axis=0)
    gate_flat = by_device(gates).reshape(-1)
    cot_rows = jnp.repeat(by_device(out_grad).reshape(devices * TOK_DEV, D), 2, axis=0)
    grad_rows = (gate_flat[:, None] * cot_rows.astype(jnp.float32)).astype(jnp.bfloat16)
    slot_count = EXPERTS * devices * CAP
    inputs = jnp.zeros((slot_count, D), jnp.bfloat16).at[flat_pos].set(normed_rows).reshape(EXPERTS, devices * CAP, D)
    cotangents = jnp.zeros((slot_count, D), jnp.bfloat16).at[flat_pos].set(grad_rows).reshape(EXPERTS, devices * CAP, D)
    expert_results = lax.map(expert_pass, (inputs, cotangents, w_gate.reshape(EXPERTS, F, D), w_up.reshape(EXPERTS, F, D), w_down.reshape(EXPERTS, F, D)))
    expert_out = expert_results[0].reshape(slot_count, D)
    picked = jnp.take(expert_out, flat_pos, axis=0)
    weighted = lax.optimization_barrier(jnp.sum((gate_flat[:, None] * picked).reshape(devices, TOK_DEV, 2, D), axis=2))
    weighted = jnp.swapaxes(weighted.reshape(N_CTX, SEQS, TOK_DEV, D), 0, 1).reshape(SEQS, LENGTH, D)
    layer_out = (mixed + weighted).astype(jnp.bfloat16)
    return (layer_out, expert_results[1].reshape(EXPERTS * F, D), expert_results[2].reshape(EXPERTS * F, D), expert_results[3].reshape(EXPERTS * F, D))
```

```python
import jax
import jax.numpy as jnp
from jax import lax
from jax.experimental import pallas as pl
from jax.experimental.pallas import tpu as pltpu
from jax.sharding import PartitionSpec as P

HEADS = 8
HD = 128
SHARDS = 4
CAP = 6
YN = 4
MSGS = 16
ROWS = YN * CAP
MESH = pl.DeviceIdType.MESH
BF = jnp.bfloat16
F32 = jnp.float32
VMEM = pl.BlockSpec(memory_space=pltpu.VMEM)
DMA = pltpu.SemaphoreType.DMA


def coords():
    c = lax.axis_index("ctx")
    e = lax.axis_index("exp")
    z = lax.div(e, 8) * 2 + lax.div(c, 4)
    return z, lax.rem(c, 4), lax.rem(lax.div(e, 2), 4), lax.rem(e, 2)


def dev(z, y, x, core):
    return {"ctx": lax.rem(z, 2) * 4 + y, "exp": lax.div(z, 2) * 8 + x * 2 + core}


def offset(k):
    t = lax.div(k, 2)
    odd = lax.rem(t, 2)
    dz = odd * lax.div(t + 1, 2) + (1 - odd) * lax.rem(8 - lax.div(t, 2), 8)
    return dz, lax.rem(k, 2)


def dest(k):
    z, y, x, core = coords()
    dz, a = offset(k)
    return dev(lax.rem(z + dz, 8), y, x + a * (3 - 2 * x), core)


def source(k):
    z, y, x, core = coords()
    dz, a = offset(k)
    return dev(lax.rem(z + 8 - dz, 8), y, x + a * (3 - 2 * x), core)


def core_mate():
    z, y, x, core = coords()
    return dev(z, y, x, 1 - core)


def x_mate():
    z, y, x, core = coords()
    return dev(z, y, x + 1 - 2 * lax.rem(x, 2), core)


def z_mate():
    z, y, x, core = coords()
    return dev(z + 1 - 2 * lax.rem(z, 2), y, x, core)


def y_peer(step):
    z, y, x, core = coords()
    return dev(z, lax.rem(y + step, 4), x, core)


def enter():
    barrier = pltpu.get_barrier_semaphore()

    def greet(device):
        pl.semaphore_signal(barrier, inc=1, device_id=device, device_id_type=MESH)

    greet(core_mate())
    greet(x_mate())
    for step in (1, 2, 3):
        greet(y_peer(step))
    lax.fori_loop(1, MSGS, lambda k, s: (greet(dest(k)), s)[1], 0)
    pl.semaphore_wait(barrier, 5 + MSGS - 1)


def remote(src, dst, send, recv, device):
    return pltpu.make_async_remote_copy(
        src_ref=src, dst_ref=dst, send_sem=send, recv_sem=recv, device_id=device, device_id_type=MESH
    )


def each(lower, upper, body):
    def step(k, carry):
        body(k)
        return carry

    lax.fori_loop(lower, upper, step, 0)


class Dispatch:
    def __init__(self, src, out, send, recv):
        self.src, self.out = src, out
        self.send, self.recv = send, recv

    def first(self, k):
        return remote(self.src.at[k], self.out.at[0, k], self.send.at[0, k], self.recv.at[0, k], dest(k))

    def to_core(self, k):
        return remote(self.out.at[0, k], self.out.at[1, k], self.send.at[1, k], self.recv.at[1, k], core_mate())

    def to_x(self, k):
        return remote(self.out.at[0, k], self.out.at[2, k], self.send.at[2, k], self.recv.at[2, k], x_mate())

    def onward(self, k):
        return remote(self.out.at[2, k], self.out.at[3, k], self.send.at[3, k], self.recv.at[3, k], core_mate())

    def start(self):
        each(1, MSGS, lambda k: self.first(k).start())
        self.out[0, 0] = self.src[0]

    def spread(self):
        self.to_core(0).start()
        self.to_x(0).start()

        def step(k):
            self.first(k).wait_recv()
            self.to_core(k).start()
            self.to_x(k).start()
            self.to_x(k - 1).wait_recv()
            self.onward(k - 1).start()

        each(1, MSGS, step)
        self.to_x(MSGS - 1).wait_recv()
        self.onward(MSGS - 1).start()

    def finish(self):
        def step(k):
            self.to_core(k).wait_recv()
            self.onward(k).wait_recv()
            self.to_core(k).wait_send()
            self.to_x(k).wait_send()
            self.onward(k).wait_send()

        each(0, MSGS, step)
        each(1, MSGS, lambda k: self.first(k).wait_send())


class Ring:
    def __init__(self, src, own, left, right, far, send, recv):
        self.up = remote(src, left, send.at[0], recv.at[0], y_peer(1))
        self.down = remote(src, right, send.at[1], recv.at[1], y_peer(3))
        self.up2 = remote(own(1, 0), far(0), send.at[2], recv.at[2], y_peer(1))
        self.down2 = remote(own(2, 1), far(1), send.at[3], recv.at[3], y_peer(3))

    def start(self):
        self.up.start()
        self.down.start()

    def middle(self):
        self.up.wait_recv()
        self.up2.start()
        self.down.wait_recv()
        self.down2.start()

    def finish(self):
        self.up2.wait_recv()
        self.down2.wait_recv()

    def drain(self):
        for copy in (self.up, self.down, self.up2, self.down2):
            copy.wait_send()


def row_ring(src, buf, send, recv):
    half = src.shape[0] // 2
    n = src.shape[0]

    def piece(block, h):
        return buf.at[pl.ds(block * n + h * half, half)]

    return Ring(
        src,
        piece,
        buf.at[pl.ds(n, n)],
        buf.at[pl.ds(2 * n, n)],
        lambda h: piece(3, h),
        send,
        recv,
    )


def kv_ring(src, buf, base, send, recv):
    return Ring(
        src,
        lambda block, h: buf.at[base + block, h],
        buf.at[base + 1],
        buf.at[base + 2],
        lambda h: buf.at[base + 3, h],
        send,
        recv,
    )


def place(chooser, tokens, scale, placed):
    width = 512

    def step(j):
        cols = pl.ds(pl.multiple_of(j * width, width), width)
        rows = jnp.dot(chooser[...], tokens[:, cols], preferred_element_type=F32)
        if scale is not None:
            rows = rows * scale[...]
        for k in range(MSGS):
            placed[k, :, cols] = rows[k * ROWS : (k + 1) * ROWS].astype(BF)

    each(0, tokens.shape[1] // width, step)


def first_kernel(
    kv, og, pos, gts, want, kvout, cot, chooser, weight,
    ogall, posall, gall, scale, placed,
    kv_s, kv_r, og_s, og_r, small_s, small_r, d_s, d_r,
):
    enter()
    small = []
    for n, (src, buf) in enumerate(((pos, posall), (gts, gall))):
        for step in (1, 2, 3):
            sem = n * 3 + step - 1
            small.append(remote(src, buf.at[step], small_s.at[sem], small_r.at[sem], y_peer(step)))
    for copy in small:
        copy.start()
    og_ring = row_ring(og, ogall, og_s, og_r)
    og_ring.start()
    zed = remote(kv, kvout.at[4], kv_s.at[0, 4], kv_r.at[0, 4], z_mate())
    zed.start()
    near = kv_ring(kv, kvout, 0, kv_s.at[0], kv_r.at[0])
    near.start()
    n = og.shape[0]
    ogall[0:n] = og[...]
    kvout[0] = kv[...]
    posall[0] = pos[...]
    gall[0] = gts[...]
    og_ring.middle()
    for copy in small:
        copy.wait_recv()
    total = jnp.zeros((MSGS * ROWS, 1), F32)
    for block, slot in ((0, 0), (1, 1), (2, 3), (3, 2)):
        shift = block * (64 * CAP)
        hit0 = want[...] == posall[slot, 0:1, :] + shift
        hit1 = want[...] == posall[slot, 1:2, :] + shift
        gate = jnp.where(hit0, gall[slot, 0:1, :], 0.0) + jnp.where(hit1, gall[slot, 1:2, :], 0.0)
        picks = jnp.where(hit0, 1.0, 0.0) + jnp.where(hit1, 1.0, 0.0)
        chooser[:, block * n : (block + 1) * n] = picks.astype(BF)
        weight[:, block * n : (block + 1) * n] = gate
        total = total + jnp.sum(gate, axis=1, keepdims=True)
    scale[...] = total
    near.middle()
    og_ring.finish()
    place(chooser, ogall, scale, placed)
    sends = Dispatch(placed, cot, d_s, d_r)
    sends.start()
    zed.wait_recv()
    other = kv_ring(kvout.at[4], kvout, 4, kv_s.at[1], kv_r.at[1])
    other.start()
    other.middle()
    near.finish()
    other.finish()
    sends.spread()
    sends.finish()
    og_ring.drain()
    near.drain()
    other.drain()
    zed.wait_send()
    for copy in small:
        copy.wait_send()


def normed_kernel(normed, chooser, out, all_rows, placed, y_s, y_r, d_s, d_r):
    enter()
    ring = row_ring(normed, all_rows, y_s, y_r)
    ring.start()
    all_rows[0 : normed.shape[0]] = normed[...]
    ring.middle()
    ring.finish()
    place(chooser, all_rows, None, placed)
    sends = Dispatch(placed, out, d_s, d_r)
    sends.start()
    sends.spread()
    sends.finish()
    ring.drain()


def return_kernel(
    parts, hi, lo, out,
    from_core, from_diag, pair, from_x, summed, back, flat, partial, peers,
    c_s, c_r, b_s, b_r, p_s, p_r,
):
    enter()

    def mate_own(k):
        return remote(parts.at[1, k], from_core.at[k], c_s.at[0, k], c_r.at[0, k], core_mate())

    def mate_diag(k):
        return remote(parts.at[3, k], from_diag.at[k], c_s.at[1, k], c_r.at[1, k], core_mate())

    def across(k):
        return remote(pair.at[k], from_x.at[k], c_s.at[2, k], c_r.at[2, k], x_mate())

    def home(k):
        return remote(summed.at[k], back.at[k], b_s.at[k], b_r.at[k], source(k))

    def begin(k):
        mate_diag(k).start()
        mate_own(k).start()

    each(0, MSGS, begin)

    def add_pair(k):
        mate_diag(k).wait_recv()
        pair[k] = (parts[2, k].astype(F32) + from_diag[k].astype(F32)).astype(BF)
        across(k).start()

    each(0, MSGS, add_pair)

    def total(k):
        mate_own(k).wait_recv()
        across(k).wait_recv()
        rows = parts[0, k].astype(F32) + from_core[k].astype(F32) + from_x[k].astype(F32)
        return rows.astype(BF)

    flat[0:ROWS] = total(0).astype(F32)

    def send_home(k):
        summed[k] = total(k)
        home(k).start()

    each(1, MSGS, send_home)

    def take(k):
        home(k).wait_recv()
        flat[pl.ds(pl.multiple_of(k * ROWS, 8), ROWS)] = back[k].astype(F32)

    each(1, MSGS, take)

    n = out.shape[0]
    width = 512
    steps = {1: 3, 2: 1, 3: 2}

    def to_peer(block):
        return remote(
            partial.at[block - 1], peers.at[block - 1], p_s.at[block - 1], p_r.at[block - 1], y_peer(steps[block])
        )

    for block in (3, 1, 2, 0):
        mine = slice(block * n, (block + 1) * n)

        def column(j):
            cols = pl.ds(pl.multiple_of(j * width, width), width)
            rows = flat[:, cols].astype(BF)
            value = jnp.dot(hi[mine], rows, preferred_element_type=F32) + jnp.dot(
                lo[mine], rows, preferred_element_type=F32
            )
            if block:
                partial[block - 1, :, cols] = value.astype(BF)
            else:
                out[:, cols] = value

        each(0, out.shape[1] // width, column)
        if block:
            to_peer(block).start()
    for block in (1, 2, 3):
        to_peer(block).wait_recv()
        out[...] += peers[block - 1].astype(F32)
    for block in (1, 2, 3):
        to_peer(block).wait_send()

    def drain(k):
        mate_diag(k).wait_send()
        mate_own(k).wait_send()
        across(k).wait_send()

    each(0, MSGS, drain)
    each(1, MSGS, lambda k: home(k).wait_send())


def call(kernel, number, outs, scratch, args):
    return pl.pallas_call(
        kernel,
        out_shape=outs,
        in_specs=[VMEM] * len(args),
        out_specs=jax.tree.map(lambda _: VMEM, outs),
        scratch_shapes=scratch,
        compiler_params=pltpu.CompilerParams(
            collective_id=number, has_side_effects=True, vmem_limit_bytes=60 << 20
        ),
    )(*args)


def per_device(
    tokens,
    queries,
    keys,
    values,
    out_proj,
    mod_scale,
    mod_shift,
    expert_ids,
    gates,
    w_gate,
    w_up,
    w_down,
    out_grad,
):
    n = tokens.shape[1]
    width = tokens.shape[2]
    inner = queries.shape[2]
    rows = MSGS * ROWS
    z, y, x, _ = coords()
    chosen = expert_ids[0].reshape(-1)
    one_hot = (chosen[:, None] == jnp.arange(64, dtype=jnp.int32)[None, :]).astype(jnp.int32)
    before = jnp.cumsum(one_hot, axis=0) - one_hot
    position = (chosen * CAP + jnp.sum(one_hot * before, axis=1)).reshape(n, 2)
    pos = jnp.pad(position.T, ((0, 6), (0, 0)))
    gts = jnp.pad(gates[0].T, ((0, 6), (0, 0)))
    row = jnp.arange(rows, dtype=jnp.int32)
    dz, a = offset(row // ROWS)
    to_z = (z + dz) % 8
    to_x = x + a * (3 - 2 * x)
    expert = ((to_z % 2) * 4 + y) * 8 + (to_z // 2) * 2 + to_x // 2
    want = (row % ROWS // CAP) * (64 * CAP) + expert * CAP + row % CAP
    want = jnp.broadcast_to(want[:, None], (rows, n))

    kv, cot, chooser, weight = call(
        first_kernel,
        1,
        (
            jax.ShapeDtypeStruct((8, 2, n, inner), BF),
            jax.ShapeDtypeStruct((4, MSGS, ROWS, width), BF),
            jax.ShapeDtypeStruct((rows, YN * n), BF),
            jax.ShapeDtypeStruct((rows, YN * n), F32),
        ),
        [
            pltpu.VMEM((YN * n, width), BF),
            pltpu.VMEM((YN, 8, n), jnp.int32),
            pltpu.VMEM((YN, 8, n), F32),
            pltpu.VMEM((rows, 1), F32),
            pltpu.VMEM((MSGS, ROWS, width), BF),
            DMA((2, 5)),
            DMA((2, 5)),
            DMA((4,)),
            DMA((4,)),
            DMA((6,)),
            DMA((6,)),
            DMA((4, MSGS)),
            DMA((4, MSGS)),
        ],
        (jnp.stack([keys[0], values[0]]), out_grad[0], pos, gts, want),
    )
    weight = weight.T
    hi = weight.astype(BF)
    lo = (weight - hi.astype(F32)).astype(BF)

    query_heads = queries[0].reshape(n, HEADS, HD)
    key_heads = kv[:, 0].reshape(8 * n, HEADS, HD)
    value_heads = kv[:, 1].reshape(8 * n, HEADS, HD)
    scores = jnp.einsum("qhd,khd->hqk", query_heads, key_heads, preferred_element_type=F32) * HD ** (-0.5)
    exponent = jnp.exp(scores - jnp.max(scores, axis=-1)[..., None])
    accum = jnp.einsum("hqk,khd->hqd", exponent.astype(BF), value_heads, preferred_element_type=F32)
    attended = (
        jnp.transpose(accum / jnp.sum(exponent, axis=-1)[..., None], (1, 0, 2)).reshape(n, inner).astype(BF)
    )
    mixed = tokens[0].astype(F32) + jnp.dot(attended, out_proj, preferred_element_type=F32)
    mean_square = jnp.mean(mixed * mixed, axis=-1, keepdims=True)
    normed = (mixed * lax.rsqrt(mean_square + 1e-06) * (1.0 + mod_scale) + mod_shift).astype(BF)

    expert_in = call(
        normed_kernel,
        2,
        jax.ShapeDtypeStruct((4, MSGS, ROWS, width), BF),
        [
            pltpu.VMEM((YN * n, width), BF),
            pltpu.VMEM((MSGS, ROWS, width), BF),
            DMA((4,)),
            DMA((4,)),
            DMA((4, MSGS)),
            DMA((4, MSGS)),
        ],
        (normed, chooser),
    )
    expert_rows = expert_in.reshape(4 * rows, width)
    row_grads = cot.reshape(4 * rows, width)
    gate_pre = jnp.einsum("rd,fd->rf", expert_rows, w_gate, preferred_element_type=F32)
    up_pre = jnp.einsum("rd,fd->rf", expert_rows, w_up, preferred_element_type=F32)
    sigmoid_gate = jax.nn.sigmoid(gate_pre)
    activation = gate_pre * sigmoid_gate
    hidden = (activation * up_pre).astype(BF)
    piece_out = jnp.einsum("rf,fd->rd", hidden, w_down, preferred_element_type=F32).astype(BF)
    block = pltpu.VMEM((MSGS, ROWS, width), BF)
    combined = call(
        return_kernel,
        3,
        jax.ShapeDtypeStruct((n, width), F32),
        [
            block,
            block,
            block,
            block,
            block,
            block,
            pltpu.VMEM((rows, width), F32),
            pltpu.VMEM((3, n, width), BF),
            pltpu.VMEM((3, n, width), BF),
            DMA((3, MSGS)),
            DMA((3, MSGS)),
            DMA((MSGS,)),
            DMA((MSGS,)),
            DMA((3,)),
            DMA((3,)),
        ],
        (piece_out.reshape(4, MSGS, ROWS, width), hi, lo),
    )
    hidden_grad = jnp.einsum("rd,fd->rf", row_grads, w_down, preferred_element_type=F32)
    gate_cot = (hidden_grad * up_pre * sigmoid_gate * (1.0 + gate_pre * (1.0 - sigmoid_gate))).astype(BF)
    up_cot = (hidden_grad * activation).astype(BF)
    grad_down = jnp.einsum("rf,rd->fd", hidden, row_grads, preferred_element_type=F32).astype(BF)
    grad_gate = jnp.einsum("rf,rd->fd", gate_cot, expert_rows, preferred_element_type=F32).astype(BF)
    grad_up = jnp.einsum("rf,rd->fd", up_cot, expert_rows, preferred_element_type=F32).astype(BF)
    layer_out = (mixed + combined).astype(BF)[None]
    return (layer_out, grad_gate, grad_up, grad_down)


def solution(mesh):
    placed = (
        P("exp", "ctx", None),
        P("exp", "ctx", None),
        P("exp", "ctx", None),
        P("exp", "ctx", None),
        P(),
        P("exp", None),
        P("exp", None),
        P("exp", "ctx", None),
        P("exp", "ctx", None),
        P(("ctx", "exp"), None),
        P(("ctx", "exp"), None),
        P(("ctx", "exp"), None),
        P("exp", "ctx", None),
    )
    return jax.shard_map(
        per_device,
        mesh=mesh,
        in_specs=placed,
        out_specs=(
            P("exp", "ctx", None),
            P(("ctx", "exp"), None),
            P(("ctx", "exp"), None),
            P(("ctx", "exp"), None),
        ),
        check_vma=False,
    )
```

```python
import jax
import jax.numpy as jnp
from jax import lax
from jax.experimental import pallas as pl
from jax.experimental.pallas import tpu as pltpu
from jax.sharding import PartitionSpec as P

HEADS = 8
HD = 128
SHARDS = 4
CAP = 6
YN = 4
MSGS = 16
ROWS = YN * CAP
MESH = pl.DeviceIdType.MESH
BF = jnp.bfloat16
F32 = jnp.float32
VMEM = pl.BlockSpec(memory_space=pltpu.VMEM)
ANY = pl.BlockSpec(memory_space=pl.ANY)
DMA = pltpu.SemaphoreType.DMA


def coords():
    c = lax.axis_index("ctx")
    e = lax.axis_index("exp")
    z = lax.div(e, 8) * 2 + lax.div(c, 4)
    return z, lax.rem(c, 4), lax.rem(lax.div(e, 2), 4), lax.rem(e, 2)


def dev(z, y, x, core):
    return {"ctx": lax.rem(z, 2) * 4 + y, "exp": lax.div(z, 2) * 8 + x * 2 + core}


def offset(k):
    t = lax.div(k, 2)
    odd = lax.rem(t, 2)
    dz = odd * lax.div(t + 1, 2) + (1 - odd) * lax.rem(8 - lax.div(t, 2), 8)
    return dz, lax.rem(k, 2)


def dest(k):
    z, y, x, core = coords()
    dz, a = offset(k)
    return dev(lax.rem(z + dz, 8), y, x + a * (3 - 2 * x), core)


def source(k):
    z, y, x, core = coords()
    dz, a = offset(k)
    return dev(lax.rem(z + 8 - dz, 8), y, x + a * (3 - 2 * x), core)


def core_mate():
    z, y, x, core = coords()
    return dev(z, y, x, 1 - core)


def x_mate():
    z, y, x, core = coords()
    return dev(z, y, x + 1 - 2 * lax.rem(x, 2), core)


def z_mate():
    z, y, x, core = coords()
    return dev(z + 1 - 2 * lax.rem(z, 2), y, x, core)


def y_peer(step):
    z, y, x, core = coords()
    return dev(z, lax.rem(y + step, 4), x, core)


def enter():
    barrier = pltpu.get_barrier_semaphore()

    def greet(device):
        pl.semaphore_signal(barrier, inc=1, device_id=device, device_id_type=MESH)

    greet(core_mate())
    greet(x_mate())
    for step in (1, 2, 3):
        greet(y_peer(step))
    lax.fori_loop(1, MSGS, lambda k, s: (greet(dest(k)), s)[1], 0)
    pl.semaphore_wait(barrier, 5 + MSGS - 1)


def remote(src, dst, send, recv, device):
    return pltpu.make_async_remote_copy(
        src_ref=src, dst_ref=dst, send_sem=send, recv_sem=recv, device_id=device, device_id_type=MESH
    )


def each(lower, upper, body):
    def step(k, carry):
        body(k)
        return carry

    lax.fori_loop(lower, upper, step, 0)


class Dispatch:
    def __init__(self, src, out, cols, send, recv, local):
        self.src, self.out, self.cols = src, out, cols
        self.send, self.recv = send, recv
        self.local = pltpu.make_async_copy(src.at[0, :, cols], out.at[0, 0, :, cols], local)

    def hop(self, stage, src, block, k, device):
        return remote(
            src, self.out.at[block, k, :, self.cols], self.send.at[stage, k], self.recv.at[stage, k], device
        )

    def first(self, k):
        return self.hop(0, self.src.at[k, :, self.cols], 0, k, dest(k))

    def to_core(self, k):
        return self.hop(1, self.out.at[0, k, :, self.cols], 1, k, core_mate())

    def to_x(self, k):
        return self.hop(2, self.out.at[0, k, :, self.cols], 2, k, x_mate())

    def onward(self, k):
        return self.hop(3, self.out.at[2, k, :, self.cols], 3, k, core_mate())

    def start(self):
        self.local.start()
        each(1, MSGS, lambda k: self.first(k).start())

    def spread_own(self):
        self.local.wait()
        self.to_core(0).start()
        self.to_x(0).start()

    def spread(self, lower, upper):
        def step(k):
            self.first(k).wait_recv()
            self.to_core(k).start()
            self.to_x(k).start()
            self.to_x(k - 1).wait_recv()
            self.onward(k - 1).start()

        each(lower, upper, step)

    def spread_last(self):
        self.to_x(MSGS - 1).wait_recv()
        self.onward(MSGS - 1).start()

    def finish(self):
        def step(k):
            self.to_core(k).wait_recv()
            self.onward(k).wait_recv()
            self.to_core(k).wait_send()
            self.to_x(k).wait_send()
            self.onward(k).wait_send()

        each(0, MSGS, step)
        each(1, MSGS, lambda k: self.first(k).wait_send())


class Ring:
    def __init__(self, src, own, left, right, far, send, recv):
        self.up = remote(src, left, send.at[0], recv.at[0], y_peer(1))
        self.down = remote(src, right, send.at[1], recv.at[1], y_peer(3))
        self.up2 = remote(own(1, 0), far(0), send.at[2], recv.at[2], y_peer(1))
        self.down2 = remote(own(2, 1), far(1), send.at[3], recv.at[3], y_peer(3))

    def start(self):
        self.up.start()
        self.down.start()

    def middle(self):
        self.up.wait_recv()
        self.up2.start()
        self.down.wait_recv()
        self.down2.start()

    def finish(self):
        self.up2.wait_recv()
        self.down2.wait_recv()

    def drain(self):
        for copy in (self.up, self.down, self.up2, self.down2):
            copy.wait_send()


def row_ring(src, buf, cols, send, recv):
    n = src.shape[0]
    half = n // 2

    def piece(block, h):
        return buf.at[pl.ds(block * n + h * half, half), cols]

    return Ring(
        src.at[:, cols],
        piece,
        buf.at[pl.ds(n, n), cols],
        buf.at[pl.ds(2 * n, n), cols],
        lambda h: piece(3, h),
        send,
        recv,
    )


def kv_ring(buf, base, send, recv):
    return Ring(
        buf.at[base],
        lambda block, h: buf.at[base + block, h],
        buf.at[base + 1],
        buf.at[base + 2],
        lambda h: buf.at[base + 3, h],
        send,
        recv,
    )


def place(chooser, tokens, scale, placed, base, size):
    width = 512

    def step(j):
        cols = pl.ds(pl.multiple_of(base + j * width, width), width)
        rows = jnp.dot(chooser[...], tokens[:, cols], preferred_element_type=F32)
        if scale is not None:
            rows = rows * scale[...]
        for k in range(MSGS):
            placed[k, :, cols] = rows[k * ROWS : (k + 1) * ROWS].astype(BF)

    each(0, size // width, step)


def attend(queries, kvall, attended, h):
    cols = pl.ds(pl.multiple_of(h * HD, HD), HD)
    keys = kvall[:, 0, :, cols].reshape(-1, HD)
    values = kvall[:, 1, :, cols].reshape(-1, HD)
    scores = lax.dot_general(
        queries[:, cols], keys, (((1,), (1,)), ((), ())), preferred_element_type=F32
    ) * HD ** (-0.5)
    exponent = jnp.exp(scores - jnp.max(scores, axis=1, keepdims=True))
    total = jnp.sum(exponent, axis=1, keepdims=True)
    mixed = jnp.dot(exponent.astype(BF), values, preferred_element_type=F32)
    attended[:, cols] = (mixed / total).astype(BF)


CHUNKS = 1


def forward_kernel(
    keys, values, out_proj, og, queries, tokens, mod, small, want,
    cot, expert_in, mixed, hi, lo,
    kvall, ogall, nall, smallall, ready, scale, placed_cot, placed_in, chooser, attended, normed, proj,
    load, local, kv_s, kv_r, og_s, og_r, small_s, small_r, n_s, n_r, c_s, c_r, d_s, d_r,
):
    n, width = og.shape
    every = pl.ds(0, width)
    key_load = pltpu.make_async_copy(keys, kvall.at[0, 0], load.at[0])
    value_load = pltpu.make_async_copy(values, kvall.at[0, 1], load.at[1])
    proj_load = pltpu.make_async_copy(out_proj, proj, load.at[2])
    key_load.start()
    value_load.start()
    proj_load.start()
    names = lax.broadcasted_iota(jnp.int32, (64, n), 0).astype(F32)
    hit0 = names == small[0:1, :]
    hit1 = names == small[1:2, :]
    earlier = lax.broadcasted_iota(jnp.int32, (n, n), 0) < lax.broadcasted_iota(jnp.int32, (n, n), 1)
    named = jnp.where(hit0, 1.0, 0.0) + jnp.where(hit1, 1.0, 0.0)
    before = jnp.dot(named.astype(BF), jnp.where(earlier, 1.0, 0.0).astype(BF), preferred_element_type=F32)
    slot0 = jnp.sum(jnp.where(hit0, before, 0.0), axis=0, keepdims=True)
    slot1 = jnp.sum(jnp.where(hit1, before, 0.0), axis=0, keepdims=True)
    ready[0:1, :] = small[0:1, :] * CAP + slot0
    ready[1:2, :] = small[1:2, :] * CAP + slot1
    ready[2:8, :] = small[2:8, :]
    enter()
    og_ring = row_ring(og, ogall, every, og_s, og_r)
    og_ring.start()
    key_load.wait()
    value_load.wait()
    zed = remote(kvall.at[0], kvall.at[4], kv_s.at[0, 4], kv_r.at[0, 4], z_mate())
    zed.start()
    near = kv_ring(kvall, 0, kv_s.at[0], kv_r.at[0])
    near.start()
    small_sends = [
        remote(ready, smallall.at[step], small_s.at[step - 1], small_r.at[step - 1], y_peer(step))
        for step in (1, 2, 3)
    ]
    for copy in small_sends:
        copy.start()
    ogall[0:n] = og[...]
    smallall[0] = ready[...]
    og_ring.middle()
    zed.wait_recv()
    other = kv_ring(kvall, 4, kv_s.at[1], kv_r.at[1])
    other.start()
    for copy in small_sends:
        copy.wait_recv()
    total = jnp.zeros((MSGS * ROWS, 1), F32)
    for block, slot in ((0, 0), (1, 1), (2, 3), (3, 2)):
        shift = float(block * 64 * CAP)
        hit0 = want[...] == smallall[slot, 0:1, :] + shift
        hit1 = want[...] == smallall[slot, 1:2, :] + shift
        gate = jnp.where(hit0, smallall[slot, 2:3, :], 0.0) + jnp.where(hit1, smallall[slot, 3:4, :], 0.0)
        picks = jnp.where(hit0, 1.0, 0.0) + jnp.where(hit1, 1.0, 0.0)
        chooser[:, block * n : (block + 1) * n] = picks.astype(BF)
        turned = gate.T
        top = turned.astype(BF)
        hi[block * n : (block + 1) * n, :] = top
        lo[block * n : (block + 1) * n, :] = (turned - top.astype(F32)).astype(BF)
        total = total + jnp.sum(gate, axis=1, keepdims=True)
    scale[...] = total
    near.middle()
    og_ring.finish()
    place(chooser, ogall, scale, placed_cot, 0, width)
    cot_sends = Dispatch(placed_cot, cot, every, c_s, c_r, local.at[0])
    cot_sends.start()
    other.middle()
    cot_sends.spread_own()
    cot_sends.spread(1, 5)
    near.finish()
    other.finish()
    each(0, HEADS // 2, lambda h: attend(queries, kvall, attended, h))
    cot_sends.spread(5, 10)
    each(HEADS // 2, HEADS, lambda h: attend(queries, kvall, attended, h))
    cot_sends.spread(10, 14)
    proj_load.wait()
    part = 512
    squares = jnp.zeros((n, 1), F32)
    for j in range(width // part):
        cols = slice(j * part, (j + 1) * part)
        value = tokens[:, cols].astype(F32) + jnp.dot(
            attended[...], proj[:, cols], preferred_element_type=F32
        )
        mixed[:, cols] = value
        squares = squares + jnp.sum(value * value, axis=1, keepdims=True)
    inverse = lax.rsqrt(squares * (1.0 / width) + 1e-06)
    size = width // CHUNKS
    rings, sends = [], []
    for chunk in range(CHUNKS):
        cols = pl.ds(chunk * size, size)
        window = slice(chunk * size, (chunk + 1) * size)
        normed[:, window] = (
            mixed[:, window] * inverse * (1.0 + mod[0:1, window]) + mod[1:2, window]
        ).astype(BF)
        ring = row_ring(normed, nall, cols, n_s.at[chunk], n_r.at[chunk])
        ring.start()
        rings.append(ring)
        sends.append(Dispatch(placed_in, expert_in, cols, d_s.at[chunk], d_r.at[chunk], local.at[1 + chunk]))
    nall[0:n] = normed[...]
    cot_sends.spread(14, 16)
    cot_sends.spread_last()
    for ring in rings:
        ring.middle()
    for chunk in range(CHUNKS):
        rings[chunk].finish()
        place(chooser, nall, None, placed_in, chunk * size, size)
        sends[chunk].start()
    for chunk in range(CHUNKS):
        sends[chunk].spread_own()
        sends[chunk].spread(1, MSGS)
        sends[chunk].spread_last()
    cot_sends.finish()
    for chunk in range(CHUNKS):
        sends[chunk].finish()
        rings[chunk].drain()
    og_ring.drain()
    near.drain()
    other.drain()
    zed.wait_send()
    for copy in small_sends:
        copy.wait_send()


PARTS = 2


def expert_kernel(
    rows_in, cots_in, w_gate, w_up, w_down, hi, lo,
    out, grad_gate, grad_up, grad_down,
    rows, cots, gate, up, hidden_t, gate_t, up_t,
    pieces, from_core, from_diag, pair, from_x, summed, back, flat, partial, peers,
    load, c_s, c_r, b_s, b_r, p_s, p_r,
):
    block_rows = MSGS * ROWS
    n, width = out.shape
    size = width // PARTS
    part = 512
    order = (3, 1, 2, 0)

    def window(block):
        return pl.ds(block * block_rows, block_rows)

    row_loads = [
        pltpu.make_async_copy(rows_in.at[window(block)], rows.at[window(block)], load.at[block])
        for block in order
    ]
    cot_load = pltpu.make_async_copy(cots_in, cots, load.at[4])
    for copy in row_loads:
        copy.start()
    cot_load.start()
    enter()

    def mate_own(c, k):
        return remote(pieces.at[c, 1, k], from_core.at[c, k], c_s.at[c, 0, k], c_r.at[c, 0, k], core_mate())

    def mate_diag(c, k):
        return remote(pieces.at[c, 3, k], from_diag.at[c, k], c_s.at[c, 1, k], c_r.at[c, 1, k], core_mate())

    def across(c, k):
        return remote(pair.at[c, k], from_x.at[c, k], c_s.at[c, 2, k], c_r.at[c, 2, k], x_mate())

    def home(c, k):
        return remote(summed.at[c, k], back.at[c, k], b_s.at[c, k], b_r.at[c, k], source(k))

    across_dims = (((1,), (1,)), ((), ()))
    for block, copy in zip(order, row_loads):
        copy.wait()
        mine = window(block)
        g = lax.dot_general(rows[mine, :], w_gate[...], across_dims, preferred_element_type=F32)
        u = lax.dot_general(rows[mine, :], w_up[...], across_dims, preferred_element_type=F32)
        gate[mine, :] = g
        up[mine, :] = u
        h = g * jax.nn.sigmoid(g) * u
        hidden = h.astype(BF)
        hidden_t[:, block * block_rows : (block + 1) * block_rows] = h.T.astype(BF)
        for j in range(width // part):
            value = jnp.dot(hidden, w_down[:, j * part : (j + 1) * part], preferred_element_type=F32)
            c, base = j * part // size, j * part % size
            for k in range(MSGS):
                pieces[c, block, k, :, base : base + part] = value[k * ROWS : (k + 1) * ROWS].astype(BF)
        if block == 3:
            for c in range(PARTS):
                each(0, MSGS, lambda k: mate_diag(c, k).start())
        if block == 1:
            for c in range(PARTS):
                each(0, MSGS, lambda k: mate_own(c, k).start())

    for c in range(PARTS):

        def add_pair(k):
            mate_diag(c, k).wait_recv()
            pair[c, k] = (pieces[c, 2, k].astype(F32) + from_diag[c, k].astype(F32)).astype(BF)
            across(c, k).start()

        each(0, MSGS, add_pair)

    cot_load.wait()
    for block in range(4):
        mine = window(block)
        hidden_grad = lax.dot_general(cots[mine, :], w_down[...], across_dims, preferred_element_type=F32)
        g = gate[mine, :]
        sg = jax.nn.sigmoid(g)
        columns = slice(block * block_rows, (block + 1) * block_rows)
        gate_t[:, columns] = (hidden_grad * up[mine, :] * sg * (1.0 + g * (1.0 - sg))).T.astype(BF)
        up_t[:, columns] = (hidden_grad * (g * sg)).T.astype(BF)

    for c in range(PARTS):
        cols = slice(c * size, (c + 1) * size)

        def total(k):
            mate_own(c, k).wait_recv()
            across(c, k).wait_recv()
            value = pieces[c, 0, k].astype(F32) + from_core[c, k].astype(F32) + from_x[c, k].astype(F32)
            return value.astype(BF)

        flat[0:ROWS, cols] = total(0).astype(F32)

        def send_home(k):
            summed[c, k] = total(k)
            home(c, k).start()

        each(1, MSGS, send_home)

    def gradients(j):
        cols = pl.ds(pl.multiple_of(j * part, part), part)
        grad_down[:, cols] = jnp.dot(hidden_t[...], cots[:, cols], preferred_element_type=F32).astype(BF)
        grad_gate[:, cols] = jnp.dot(gate_t[...], rows[:, cols], preferred_element_type=F32).astype(BF)
        grad_up[:, cols] = jnp.dot(up_t[...], rows[:, cols], preferred_element_type=F32).astype(BF)

    each(0, width // part, gradients)

    steps = {1: 3, 2: 1, 3: 2}

    def to_peer(c, block):
        b = block - 1
        return remote(partial.at[c, b], peers.at[c, b], p_s.at[c, b], p_r.at[c, b], y_peer(steps[block]))

    for c in range(PARTS):
        cols = slice(c * size, (c + 1) * size)

        def take(k):
            home(c, k).wait_recv()
            flat[pl.ds(pl.multiple_of(k * ROWS, 8), ROWS), cols] = back[c, k].astype(F32)

        each(1, MSGS, take)
        for block in (3, 1, 2, 0):
            mine = slice(block * n, (block + 1) * n)
            for j in range(size // part):
                at = c * size + j * part
                values = flat[:, at : at + part].astype(BF)
                value = jnp.dot(hi[mine], values, preferred_element_type=F32) + jnp.dot(
                    lo[mine], values, preferred_element_type=F32
                )
                if block:
                    partial[c, block - 1, :, j * part : (j + 1) * part] = value.astype(BF)
                else:
                    out[:, at : at + part] = value
            if block:
                to_peer(c, block).start()
    for c in range(PARTS):
        cols = slice(c * size, (c + 1) * size)
        for block in (1, 2, 3):
            to_peer(c, block).wait_recv()
            out[:, cols] += peers[c, block - 1].astype(F32)
    for c in range(PARTS):
        for block in (1, 2, 3):
            to_peer(c, block).wait_send()

        def drain(k):
            mate_diag(c, k).wait_send()
            mate_own(c, k).wait_send()
            across(c, k).wait_send()

        each(0, MSGS, drain)
        each(1, MSGS, lambda k: home(c, k).wait_send())


def call(kernel, number, outs, scratch, args, in_specs=None, out_specs=None):
    return pl.pallas_call(
        kernel,
        out_shape=outs,
        in_specs=in_specs or [VMEM] * len(args),
        out_specs=out_specs or jax.tree.map(lambda _: VMEM, outs),
        scratch_shapes=scratch,
        compiler_params=pltpu.CompilerParams(
            collective_id=number, has_side_effects=True, vmem_limit_bytes=67043328
        ),
    )(*args)


def per_device(
    tokens,
    queries,
    keys,
    values,
    out_proj,
    mod_scale,
    mod_shift,
    expert_ids,
    gates,
    w_gate,
    w_up,
    w_down,
    out_grad,
):
    n = tokens.shape[1]
    width = tokens.shape[2]
    inner = queries.shape[2]
    rows = MSGS * ROWS
    z, y, x, _ = coords()
    small = jnp.concatenate(
        [expert_ids[0].T.astype(F32), gates[0].T, jnp.zeros((4, n), F32)], axis=0
    )
    row = jnp.arange(rows, dtype=jnp.int32)
    dz, a = offset(row // ROWS)
    to_z = (z + dz) % 8
    to_x = x + a * (3 - 2 * x)
    expert = ((to_z % 2) * 4 + y) * 8 + (to_z // 2) * 2 + to_x // 2
    want = (row % ROWS // CAP) * (64 * CAP) + expert * CAP + row % CAP
    want = jnp.broadcast_to(want.astype(F32)[:, None], (rows, n))
    mod = jnp.concatenate([mod_scale, mod_shift], axis=0)

    slots = jax.ShapeDtypeStruct((4, MSGS, ROWS, width), BF)
    routed = jax.ShapeDtypeStruct((YN * n, rows), BF)
    cot, expert_in, mixed, hi, lo = call(
        forward_kernel,
        1,
        (slots, slots, jax.ShapeDtypeStruct((n, width), F32), routed, routed),
        [
            pltpu.VMEM((8, 2, n, inner), BF),
            pltpu.VMEM((YN * n, width), BF),
            pltpu.VMEM((YN * n, width), BF),
            pltpu.VMEM((YN, 8, n), F32),
            pltpu.VMEM((8, n), F32),
            pltpu.VMEM((rows, 1), F32),
            pltpu.VMEM((MSGS, ROWS, width), BF),
            pltpu.VMEM((MSGS, ROWS, width), BF),
            pltpu.VMEM((rows, YN * n), BF),
            pltpu.VMEM((n, inner), BF),
            pltpu.VMEM((n, width), BF),
            pltpu.VMEM((inner, width), BF),
            DMA((3,)),
            DMA((1 + CHUNKS,)),
            DMA((2, 5)),
            DMA((2, 5)),
            DMA((4,)),
            DMA((4,)),
            DMA((3,)),
            DMA((3,)),
            DMA((CHUNKS, 4)),
            DMA((CHUNKS, 4)),
            DMA((4, MSGS)),
            DMA((4, MSGS)),
            DMA((CHUNKS, 4, MSGS)),
            DMA((CHUNKS, 4, MSGS)),
        ],
        (keys[0], values[0], out_proj, out_grad[0], queries[0], tokens[0], mod, small, want),
        in_specs=[ANY] * 3 + [VMEM] * 6,
        out_specs=(ANY, ANY, VMEM, VMEM, VMEM),
    )
    everything = 4 * rows
    hid = w_gate.shape[0]
    block = pltpu.VMEM((PARTS, MSGS, ROWS, width // PARTS), BF)
    share = pltpu.VMEM((PARTS, 3, n, width // PARTS), BF)
    grad = jax.ShapeDtypeStruct((hid, width), BF)
    combined, grad_gate, grad_up, grad_down = call(
        expert_kernel,
        2,
        (jax.ShapeDtypeStruct((n, width), F32), grad, grad, grad),
        [
            pltpu.VMEM((everything, width), BF),
            pltpu.VMEM((everything, width), BF),
            pltpu.VMEM((everything, hid), F32),
            pltpu.VMEM((everything, hid), F32),
            pltpu.VMEM((hid, everything), BF),
            pltpu.VMEM((hid, everything), BF),
            pltpu.VMEM((hid, everything), BF),
            pltpu.VMEM((PARTS, 4, MSGS, ROWS, width // PARTS), BF),
            block,
            block,
            block,
            block,
            block,
            block,
            pltpu.VMEM((rows, width), F32),
            share,
            share,
            DMA((5,)),
            DMA((PARTS, 3, MSGS)),
            DMA((PARTS, 3, MSGS)),
            DMA((PARTS, MSGS)),
            DMA((PARTS, MSGS)),
            DMA((PARTS, 3)),
            DMA((PARTS, 3)),
        ],
        (expert_in.reshape(everything, width), cot.reshape(everything, width), w_gate, w_up, w_down, hi, lo),
        in_specs=[ANY] * 2 + [VMEM] * 5,
    )
    layer_out = (mixed + combined).astype(BF)[None]
    return (layer_out, grad_gate, grad_up, grad_down)


def solution(mesh):
    placed = (
        P("exp", "ctx", None),
        P("exp", "ctx", None),
        P("exp", "ctx", None),
        P("exp", "ctx", None),
        P(),
        P("exp", None),
        P("exp", None),
        P("exp", "ctx", None),
        P("exp", "ctx", None),
        P(("ctx", "exp"), None),
        P(("ctx", "exp"), None),
        P(("ctx", "exp"), None),
        P("exp", "ctx", None),
    )
    return jax.shard_map(
        per_device,
        mesh=mesh,
        in_specs=placed,
        out_specs=(
            P("exp", "ctx", None),
            P(("ctx", "exp"), None),
            P(("ctx", "exp"), None),
            P(("ctx", "exp"), None),
        ),
        check_vma=False,
    )
```

```python
import jax
import jax.numpy as jnp
from jax import lax
from jax.experimental import pallas as pl
from jax.experimental.pallas import tpu as pltpu
from jax.sharding import PartitionSpec as P

HEADS = 8
HD = 128
SHARDS = 4
CAP = 6
YN = 4
MSGS = 16
ROWS = YN * CAP
LAG = 3
MESH = pl.DeviceIdType.MESH
BF = jnp.bfloat16
F32 = jnp.float32
VMEM = pl.BlockSpec(memory_space=pltpu.VMEM)
ANY = pl.BlockSpec(memory_space=pl.ANY)
DMA = pltpu.SemaphoreType.DMA


def coords():
    c = lax.axis_index("ctx")
    e = lax.axis_index("exp")
    z = lax.div(e, 8) * 2 + lax.div(c, 4)
    return z, lax.rem(c, 4), lax.rem(lax.div(e, 2), 4), lax.rem(e, 2)


def dev(z, y, x, core):
    return {"ctx": lax.rem(z, 2) * 4 + y, "exp": lax.div(z, 2) * 8 + x * 2 + core}


def offset(k):
    t = lax.rem(k, 4)
    return 2 * (t + lax.div(t, 2) * (1 - 2 * lax.rem(t, 2))), lax.div(k, 4)


def dest(k):
    z, y, x, core = coords()
    dz, dy = offset(k)
    return dev(lax.rem(z + dz, 8), lax.rem(y + dy, 4), x + core * (3 - 2 * x), 1 - core)


def source(k):
    z, y, x, core = coords()
    dz, dy = offset(k)
    return dev(lax.rem(z + 8 - dz, 8), lax.rem(y + 4 - dy, 4), x + (1 - core) * (3 - 2 * x), 1 - core)


def core_mate():
    z, y, x, core = coords()
    return dev(z, y, x, 1 - core)


def x_mate():
    z, y, x, core = coords()
    return dev(z, y, x + 1 - 2 * lax.rem(x, 2), core)


def z_mate():
    z, y, x, core = coords()
    return dev(z + 1 - 2 * lax.rem(z, 2), y, x, core)


def diagonal():
    z, y, x, core = coords()
    return dev(z + 1 - 2 * lax.rem(z, 2), y, x, 1 - core)


def y_peer(step):
    z, y, x, core = coords()
    return dev(z, lax.rem(y + step, 4), x, core)


def enter():
    barrier = pltpu.get_barrier_semaphore()

    def greet(device):
        pl.semaphore_signal(barrier, inc=1, device_id=device, device_id_type=MESH)

    greet(core_mate())
    greet(x_mate())
    greet(z_mate())
    greet(diagonal())
    greet(y_peer(1))
    greet(y_peer(3))

    def far(k):
        greet(dest(k))
        greet(source(k))

    each(0, MSGS, far)
    pl.semaphore_wait(barrier, 6 + 2 * MSGS)


def remote(src, dst, send, recv, device):
    return pltpu.make_async_remote_copy(
        src_ref=src, dst_ref=dst, send_sem=send, recv_sem=recv, device_id=device, device_id_type=MESH
    )


def each(lower, upper, body):
    def step(k, carry):
        body(k)
        return carry

    lax.fori_loop(lower, upper, step, 0)


class Dispatch:
    def __init__(self, src, out, send, recv):
        self.src, self.out = src, out
        self.send, self.recv = send, recv

    def hop(self, stage, src, block, k, device):
        return remote(
            src, self.out.at[block, k], self.send.at[stage, k], self.recv.at[stage, k], device
        )

    def first(self, k):
        return self.hop(0, self.src.at[k], 0, k, dest(k))

    def to_core(self, k):
        return self.hop(1, self.out.at[0, k], 1, k, core_mate())

    def to_x(self, k):
        return self.hop(2, self.out.at[0, k], 2, k, x_mate())

    def onward(self, k):
        return self.hop(3, self.out.at[2, k], 3, k, core_mate())

    def start(self):
        each(0, MSGS, lambda k: self.first(k).start())

    def arrive(self, k):
        self.first(k).wait_recv()
        self.to_core(k).start()
        self.to_x(k).start()

    def pass_on(self, k):
        self.to_x(k).wait_recv()
        self.onward(k).start()

    def step(self, k):
        self.arrive(k)
        self.pass_on(k - LAG)

    def spread(self, lower, upper):
        for k in range(lower, min(upper, LAG)):
            self.arrive(k)
        each(max(lower, LAG), upper, self.step)

    def spread_last(self):
        each(MSGS - LAG, MSGS, self.pass_on)

    def finish(self):
        def step(k):
            self.to_core(k).wait_recv()
            self.onward(k).wait_recv()
            self.to_core(k).wait_send()
            self.to_x(k).wait_send()
            self.onward(k).wait_send()

            self.first(k).wait_send()

        each(0, MSGS, step)


class Ring:
    def __init__(self, src, own, left, right, far, send, recv):
        self.up = remote(src, left, send.at[0], recv.at[0], y_peer(1))
        self.down = remote(src, right, send.at[1], recv.at[1], y_peer(3))
        self.up2 = remote(own(1, 0), far(0), send.at[2], recv.at[2], y_peer(1))
        self.down2 = remote(own(2, 1), far(1), send.at[3], recv.at[3], y_peer(3))

    def start(self):
        self.up.start()
        self.down.start()

    def middle(self):
        self.up.wait_recv()
        self.up2.start()
        self.down.wait_recv()
        self.down2.start()

    def finish(self):
        self.up2.wait_recv()
        self.down2.wait_recv()

    def drain(self):
        for copy in (self.up, self.down, self.up2, self.down2):
            copy.wait_send()


class Quad:
    def __init__(self, src, buf, send, recv):
        n = src.shape[0]
        self.mate = remote(src, buf.at[pl.ds(n, n)], send.at[0], recv.at[0], core_mate())
        self.zed = remote(src, buf.at[pl.ds(2 * n, n)], send.at[1], recv.at[1], z_mate())
        self.far = remote(
            buf.at[pl.ds(2 * n, n)], buf.at[pl.ds(3 * n, n)], send.at[2], recv.at[2], core_mate()
        )

    def start(self):
        self.zed.start()
        self.mate.start()

    def middle(self):
        self.zed.wait_recv()
        self.far.start()

    def finish(self):
        self.mate.wait_recv()
        self.far.wait_recv()

    def drain(self):
        for copy in (self.mate, self.zed, self.far):
            copy.wait_send()


def kv_ring(buf, base, send, recv):
    return Ring(
        buf.at[base],
        lambda block, h: buf.at[base + block, h],
        buf.at[base + 1],
        buf.at[base + 2],
        lambda h: buf.at[base + 3, h],
        send,
        recv,
    )


def place(chooser, tokens, scale, placed):
    width = 512

    def step(j):
        cols = pl.ds(pl.multiple_of(j * width, width), width)
        rows = jnp.dot(chooser[...], tokens[:, cols], preferred_element_type=F32)
        if scale is not None:
            rows = rows * scale[...]
        for k in range(MSGS):
            placed[k, :, cols] = rows[k * ROWS : (k + 1) * ROWS].astype(BF)

    each(0, tokens.shape[1] // width, step)


def attend(queries, kvall, attended, h):
    cols = pl.ds(pl.multiple_of(h * HD, HD), HD)
    keys = kvall[:, 0, :, cols].reshape(-1, HD)
    values = kvall[:, 1, :, cols].reshape(-1, HD)
    scores = lax.dot_general(
        queries[:, cols], keys, (((1,), (1,)), ((), ())), preferred_element_type=F32
    ) * HD ** (-0.5)
    exponent = jnp.exp(scores - jnp.max(scores, axis=1, keepdims=True))
    total = jnp.sum(exponent, axis=1, keepdims=True)
    mixed = jnp.dot(exponent.astype(BF), values, preferred_element_type=F32)
    attended[:, cols] = (mixed / total).astype(BF)


def forward_kernel(
    keys, values, out_proj, og, queries, tokens, mod, small, want,
    cot, expert_in, mixed, hi, lo,
    kvall, ogall, nall, smallall, ready, scale, placed_cot, placed_in, chooser, attended, normed, proj,
    load, kv_s, kv_r, og_s, og_r, small_s, small_r, n_s, n_r, c_s, c_r, d_s, d_r,
):
    n, width = og.shape
    key_load = pltpu.make_async_copy(keys, kvall.at[0, 0], load.at[0])
    value_load = pltpu.make_async_copy(values, kvall.at[0, 1], load.at[1])
    proj_load = pltpu.make_async_copy(out_proj, proj, load.at[2])
    key_load.start()
    value_load.start()
    proj_load.start()
    names = lax.broadcasted_iota(jnp.int32, (64, n), 0).astype(F32)
    hit0 = names == small[0:1, :]
    hit1 = names == small[1:2, :]
    earlier = lax.broadcasted_iota(jnp.int32, (n, n), 0) < lax.broadcasted_iota(jnp.int32, (n, n), 1)
    named = jnp.where(hit0, 1.0, 0.0) + jnp.where(hit1, 1.0, 0.0)
    before = jnp.dot(named.astype(BF), jnp.where(earlier, 1.0, 0.0).astype(BF), preferred_element_type=F32)
    slot0 = jnp.sum(jnp.where(hit0, before, 0.0), axis=0, keepdims=True)
    slot1 = jnp.sum(jnp.where(hit1, before, 0.0), axis=0, keepdims=True)
    ready[0:1, :] = small[0:1, :] * CAP + slot0
    ready[1:2, :] = small[1:2, :] * CAP + slot1
    ready[2:8, :] = small[2:8, :]
    enter()
    small_sends = [
        remote(ready, smallall.at[s], small_s.at[s - 1], small_r.at[s - 1], device)
        for s, device in ((1, core_mate()), (2, z_mate()), (3, diagonal()))
    ]
    for copy in small_sends:
        copy.start()
    og_quad = Quad(og, ogall, og_s, og_r)
    og_quad.start()
    key_load.wait()
    value_load.wait()
    near = kv_ring(kvall, 0, kv_s.at[0], kv_r.at[0])
    near.start()
    zed = remote(kvall.at[0], kvall.at[4], kv_s.at[0, 4], kv_r.at[0, 4], z_mate())
    zed.start()
    ogall[0:n] = og[...]
    smallall[0] = ready[...]
    for copy in small_sends:
        copy.wait_recv()
    total = jnp.zeros((MSGS * ROWS, 1), F32)
    for block in range(4):
        shift = float(block * 64 * CAP)
        hit0 = want[...] == smallall[block, 0:1, :] + shift
        hit1 = want[...] == smallall[block, 1:2, :] + shift
        gate = jnp.where(hit0, smallall[block, 2:3, :], 0.0) + jnp.where(hit1, smallall[block, 3:4, :], 0.0)
        picks = jnp.where(hit0, 1.0, 0.0) + jnp.where(hit1, 1.0, 0.0)
        chooser[:, block * n : (block + 1) * n] = picks.astype(BF)
        turned = gate.T
        top = turned.astype(BF)
        hi[block * n : (block + 1) * n, :] = top
        lo[block * n : (block + 1) * n, :] = (turned - top.astype(F32)).astype(BF)
        total = total + jnp.sum(gate, axis=1, keepdims=True)
    scale[...] = total
    og_quad.middle()
    near.middle()
    og_quad.finish()
    place(chooser, ogall, scale, placed_cot)
    cot_sends = Dispatch(placed_cot, cot, c_s, c_r)
    cot_sends.start()
    zed.wait_recv()
    other = kv_ring(kvall, 4, kv_s.at[1], kv_r.at[1])
    other.start()
    cot_sends.spread(0, 2)
    other.middle()
    cot_sends.spread(2, 5)
    near.finish()
    other.finish()

    def attend_and_spread(h):
        attend(queries, kvall, attended, h)
        cot_sends.step(h + 5)

    each(0, HEADS, attend_and_spread)
    proj_load.wait()
    part = 512
    squares = jnp.zeros((n, 1), F32)
    for j in range(width // part):
        cols = slice(j * part, (j + 1) * part)
        value = tokens[:, cols].astype(F32) + jnp.dot(
            attended[...], proj[:, cols], preferred_element_type=F32
        )
        mixed[:, cols] = value
        squares = squares + jnp.sum(value * value, axis=1, keepdims=True)
    inverse = lax.rsqrt(squares * (1.0 / width) + 1e-06)
    normed[...] = (mixed[...] * inverse * (1.0 + mod[0:1, :]) + mod[1:2, :]).astype(BF)
    quad = Quad(normed, nall, n_s, n_r)
    quad.start()
    nall[0:n] = normed[...]
    cot_sends.spread(13, 16)
    cot_sends.spread_last()
    quad.middle()
    quad.finish()
    place(chooser, nall, None, placed_in)
    sends = Dispatch(placed_in, expert_in, d_s, d_r)
    sends.start()
    sends.spread(0, MSGS)
    sends.spread_last()
    cot_sends.finish()
    sends.finish()
    quad.drain()
    og_quad.drain()
    near.drain()
    other.drain()
    zed.wait_send()
    for copy in small_sends:
        copy.wait_send()


PARTS = 2


def expert_kernel(
    rows_in, cots_in, w_gate, w_up, w_down, hi, lo,
    out, grad_gate, grad_up, grad_down,
    rows, cots, gate, up, hidden_t, gate_t, up_t,
    pieces, from_core, from_diag, pair, from_x, summed, back, flat, middle, partial, peers,
    load, c_s, c_r, b_s, b_r, p_s, p_r,
):
    block_rows = MSGS * ROWS
    n, width = out.shape
    size = width // PARTS
    part = 512
    order = (3, 1, 2, 0)

    def window(block):
        return pl.ds(block * block_rows, block_rows)

    row_loads = [
        pltpu.make_async_copy(rows_in.at[window(block)], rows.at[window(block)], load.at[block])
        for block in order
    ]
    cot_load = pltpu.make_async_copy(cots_in, cots, load.at[4])
    for copy in row_loads:
        copy.start()
    cot_load.start()
    enter()

    def mate_own(c, k):
        return remote(pieces.at[c, 1, k], from_core.at[c, k], c_s.at[c, 0, k], c_r.at[c, 0, k], core_mate())

    def mate_diag(c, k):
        return remote(pieces.at[c, 3, k], from_diag.at[c, k], c_s.at[c, 1, k], c_r.at[c, 1, k], core_mate())

    def across(c, k):
        return remote(pair.at[c, k], from_x.at[c, k], c_s.at[c, 2, k], c_r.at[c, 2, k], x_mate())

    def home(c, k):
        return remote(summed.at[c, k], back.at[c, k], b_s.at[c, k], b_r.at[c, k], source(k))

    across_dims = (((1,), (1,)), ((), ()))
    for block, copy in zip(order, row_loads):
        copy.wait()
        mine = window(block)
        g = lax.dot_general(rows[mine, :], w_gate[...], across_dims, preferred_element_type=F32)
        u = lax.dot_general(rows[mine, :], w_up[...], across_dims, preferred_element_type=F32)
        gate[mine, :] = g
        up[mine, :] = u
        h = g * jax.nn.sigmoid(g) * u
        hidden = h.astype(BF)
        hidden_t[:, block * block_rows : (block + 1) * block_rows] = h.T.astype(BF)
        for j in range(width // part):
            value = jnp.dot(hidden, w_down[:, j * part : (j + 1) * part], preferred_element_type=F32)
            c, base = j * part // size, j * part % size
            for k in range(MSGS):
                pieces[c, block, k, :, base : base + part] = value[k * ROWS : (k + 1) * ROWS].astype(BF)
        if block == 3:
            for c in range(PARTS):
                each(0, MSGS, lambda k: mate_diag(c, k).start())
        if block == 1:
            for c in range(PARTS):
                each(0, MSGS, lambda k: mate_own(c, k).start())

    for c in range(PARTS):

        def add_pair(k):
            mate_diag(c, k).wait_recv()
            pair[c, k] = (pieces[c, 2, k].astype(F32) + from_diag[c, k].astype(F32)).astype(BF)
            across(c, k).start()

        each(0, MSGS, add_pair)

    cot_load.wait()
    for block in range(4):
        mine = window(block)
        hidden_grad = lax.dot_general(cots[mine, :], w_down[...], across_dims, preferred_element_type=F32)
        g = gate[mine, :]
        sg = jax.nn.sigmoid(g)
        columns = slice(block * block_rows, (block + 1) * block_rows)
        gate_t[:, columns] = (hidden_grad * up[mine, :] * sg * (1.0 + g * (1.0 - sg))).T.astype(BF)
        up_t[:, columns] = (hidden_grad * (g * sg)).T.astype(BF)

    for c in range(PARTS):
        cols = slice(c * size, (c + 1) * size)

        def total(k):
            mate_own(c, k).wait_recv()
            across(c, k).wait_recv()
            value = pieces[c, 0, k].astype(F32) + from_core[c, k].astype(F32) + from_x[c, k].astype(F32)
            return value.astype(BF)

        def send_home(k):
            summed[c, k] = total(k)
            home(c, k).start()

        each(0, MSGS, send_home)

    def gradients(j):
        cols = pl.ds(pl.multiple_of(j * part, part), part)
        grad_down[:, cols] = jnp.dot(hidden_t[...], cots[:, cols], preferred_element_type=F32).astype(BF)
        grad_gate[:, cols] = jnp.dot(gate_t[...], rows[:, cols], preferred_element_type=F32).astype(BF)
        grad_up[:, cols] = jnp.dot(up_t[...], rows[:, cols], preferred_element_type=F32).astype(BF)

    each(0, width // part, gradients)

    def to_peer(c, block):
        b = block - 1
        device = z_mate() if block == 2 else core_mate()
        return remote(partial.at[c, b], peers.at[c, b], p_s.at[c, b], p_r.at[c, b], device)

    for c in range(PARTS):
        cols = slice(c * size, (c + 1) * size)

        def take(k):
            home(c, k).wait_recv()
            flat[pl.ds(pl.multiple_of(k * ROWS, 8), ROWS), cols] = back[c, k].astype(F32)

        each(0, MSGS, take)
        for block in (3, 2, 1, 0):
            mine = slice(block * n, (block + 1) * n)
            for j in range(size // part):
                at = c * size + j * part
                values = flat[:, at : at + part].astype(BF)
                value = jnp.dot(hi[mine], values, preferred_element_type=F32) + jnp.dot(
                    lo[mine], values, preferred_element_type=F32
                )
                here = slice(j * part, (j + 1) * part)
                if block == 2:
                    middle[c, :, here] = value
                elif block:
                    partial[c, block - 1, :, here] = value.astype(BF)
                else:
                    out[:, at : at + part] = value
            if block == 3 or block == 1:
                to_peer(c, block).start()
            if block == 1:
                to_peer(c, 3).wait_recv()
                partial[c, 1] = (middle[c] + peers[c, 2].astype(F32)).astype(BF)
                to_peer(c, 2).start()
    for c in range(PARTS):
        cols = slice(c * size, (c + 1) * size)
        for block in (1, 2):
            to_peer(c, block).wait_recv()
            out[:, cols] += peers[c, block - 1].astype(F32)
    for c in range(PARTS):
        for block in (1, 2, 3):
            to_peer(c, block).wait_send()

        def drain(k):
            mate_diag(c, k).wait_send()
            mate_own(c, k).wait_send()
            across(c, k).wait_send()
            home(c, k).wait_send()

        each(0, MSGS, drain)


def finish_kernel(mixed, combined, a, b, c, out, a_out, b_out, c_out):
    out[...] = (mixed[...] + combined[...]).astype(BF)
    a_out[...] = a[...]
    b_out[...] = b[...]
    c_out[...] = c[...]


def call(kernel, number, outs, scratch, args, in_specs=None, out_specs=None):
    return pl.pallas_call(
        kernel,
        out_shape=outs,
        in_specs=in_specs or [VMEM] * len(args),
        out_specs=out_specs or jax.tree.map(lambda _: VMEM, outs),
        scratch_shapes=scratch,
        compiler_params=pltpu.CompilerParams(
            collective_id=number, has_side_effects=True, vmem_limit_bytes=67043328
        ),
    )(*args)


def per_device(
    tokens,
    queries,
    keys,
    values,
    out_proj,
    mod_scale,
    mod_shift,
    expert_ids,
    gates,
    w_gate,
    w_up,
    w_down,
    out_grad,
):
    n = tokens.shape[1]
    width = tokens.shape[2]
    inner = queries.shape[2]
    rows = MSGS * ROWS
    z, y, x, core = coords()
    small = jnp.concatenate(
        [expert_ids[0].T.astype(F32), gates[0].T, jnp.zeros((4, n), F32)], axis=0
    )
    row = jnp.arange(rows, dtype=jnp.int32)
    dz, dy = offset(row // ROWS)
    to_z = (z + dz) % 8
    to_x = x + core * (3 - 2 * x)
    expert = ((to_z % 2) * 4 + (y + dy) % 4) * 8 + (to_z // 2) * 2 + to_x // 2
    want = (row % ROWS // CAP) * (64 * CAP) + expert * CAP + row % CAP
    want = jnp.broadcast_to(want.astype(F32)[:, None], (rows, n))
    mod = jnp.concatenate([mod_scale, mod_shift], axis=0)

    slots = jax.ShapeDtypeStruct((4, MSGS, ROWS, width), BF)
    routed = jax.ShapeDtypeStruct((YN * n, rows), BF)
    cot, expert_in, mixed, hi, lo = call(
        forward_kernel,
        1,
        (slots, slots, jax.ShapeDtypeStruct((n, width), F32), routed, routed),
        [
            pltpu.VMEM((8, 2, n, inner), BF),
            pltpu.VMEM((YN * n, width), BF),
            pltpu.VMEM((YN * n, width), BF),
            pltpu.VMEM((YN, 8, n), F32),
            pltpu.VMEM((8, n), F32),
            pltpu.VMEM((rows, 1), F32),
            pltpu.VMEM((MSGS, ROWS, width), BF),
            pltpu.VMEM((MSGS, ROWS, width), BF),
            pltpu.VMEM((rows, YN * n), BF),
            pltpu.VMEM((n, inner), BF),
            pltpu.VMEM((n, width), BF),
            pltpu.VMEM((inner, width), BF),
            DMA((3,)),
            DMA((2, 5)),
            DMA((2, 5)),
            DMA((3,)),
            DMA((3,)),
            DMA((3,)),
            DMA((3,)),
            DMA((3,)),
            DMA((3,)),
            DMA((4, MSGS)),
            DMA((4, MSGS)),
            DMA((4, MSGS)),
            DMA((4, MSGS)),
        ],
        (keys[0], values[0], out_proj, out_grad[0], queries[0], tokens[0], mod, small, want),
        in_specs=[ANY] * 3 + [VMEM] * 6,
        out_specs=(ANY, ANY, VMEM, VMEM, VMEM),
    )
    everything = 4 * rows
    hid = w_gate.shape[0]
    block = pltpu.VMEM((PARTS, MSGS, ROWS, width // PARTS), BF)
    share = pltpu.VMEM((PARTS, 3, n, width // PARTS), BF)
    grad = jax.ShapeDtypeStruct((hid, width), BF)
    combined, grad_gate, grad_up, grad_down = call(
        expert_kernel,
        2,
        (jax.ShapeDtypeStruct((n, width), F32), grad, grad, grad),
        [
            pltpu.VMEM((everything, width), BF),
            pltpu.VMEM((everything, width), BF),
            pltpu.VMEM((everything, hid), F32),
            pltpu.VMEM((everything, hid), F32),
            pltpu.VMEM((hid, everything), BF),
            pltpu.VMEM((hid, everything), BF),
            pltpu.VMEM((hid, everything), BF),
            pltpu.VMEM((PARTS, 4, MSGS, ROWS, width // PARTS), BF),
            block,
            block,
            block,
            block,
            block,
            block,
            pltpu.VMEM((rows, width), F32),
            pltpu.VMEM((PARTS, n, width // PARTS), F32),
            share,
            share,
            DMA((5,)),
            DMA((PARTS, 3, MSGS)),
            DMA((PARTS, 3, MSGS)),
            DMA((PARTS, MSGS)),
            DMA((PARTS, MSGS)),
            DMA((PARTS, 3)),
            DMA((PARTS, 3)),
        ],
        (expert_in.reshape(everything, width), cot.reshape(everything, width), w_gate, w_up, w_down, hi, lo),
        in_specs=[ANY] * 2 + [VMEM] * 5,
    )
    steps = 4
    thin = pl.BlockSpec((n // steps, width), lambda i: (i, 0))
    thick = pl.BlockSpec((hid // steps, width), lambda i: (i, 0))
    layer_out, grad_gate, grad_up, grad_down = pl.pallas_call(
        finish_kernel,
        grid=(steps,),
        in_specs=[thin, thin, thick, thick, thick],
        out_specs=(thin, thick, thick, thick),
        out_shape=(jax.ShapeDtypeStruct((n, width), BF), grad, grad, grad),
    )(mixed, combined, grad_gate, grad_up, grad_down)
    return (layer_out[None], grad_gate, grad_up, grad_down)


def solution(mesh):
    placed = (
        P("exp", "ctx", None),
        P("exp", "ctx", None),
        P("exp", "ctx", None),
        P("exp", "ctx", None),
        P(),
        P("exp", None),
        P("exp", None),
        P("exp", "ctx", None),
        P("exp", "ctx", None),
        P(("ctx", "exp"), None),
        P(("ctx", "exp"), None),
        P(("ctx", "exp"), None),
        P("exp", "ctx", None),
    )
    return jax.shard_map(
        per_device,
        mesh=mesh,
        in_specs=placed,
        out_specs=(
            P("exp", "ctx", None),
            P(("ctx", "exp"), None),
            P(("ctx", "exp"), None),
            P(("ctx", "exp"), None),
        ),
        check_vma=False,
    )
```

```python
import jax
import jax.numpy as jnp
from jax import lax
from jax.experimental import pallas as pl
from jax.experimental.pallas import tpu as pltpu
from jax.sharding import PartitionSpec as P

HEADS = 8
HD = 128
SHARDS = 4
CAP = 6
YN = 4
MSGS = 16
ROWS = YN * CAP
LAG = 3
MESH = pl.DeviceIdType.MESH
BF = jnp.bfloat16
F32 = jnp.float32
VMEM = pl.BlockSpec(memory_space=pltpu.VMEM)
ANY = pl.BlockSpec(memory_space=pl.ANY)
DMA = pltpu.SemaphoreType.DMA


def coords():
    c = lax.axis_index("ctx")
    e = lax.axis_index("exp")
    z = lax.div(e, 8) * 2 + lax.div(c, 4)
    return z, lax.rem(c, 4), lax.rem(lax.div(e, 2), 4), lax.rem(e, 2)


def dev(z, y, x, core):
    return {"ctx": lax.rem(z, 2) * 4 + y, "exp": lax.div(z, 2) * 8 + x * 2 + core}


def offset(k, core):
    t = lax.rem(k, 4)
    return 2 * (t + lax.div(t, 2) * (1 - 2 * lax.rem(t, 2))) + core, lax.div(k, 4)


def dest(k):
    z, y, x, core = coords()
    dz, dy = offset(k, core)
    return dev(lax.rem(z + dz, 8), lax.rem(y + dy, 4), x, 1 - core)


def source(k):
    z, y, x, core = coords()
    dz, dy = offset(k, 1 - core)
    return dev(lax.rem(z + 8 - dz, 8), lax.rem(y + 4 - dy, 4), x, 1 - core)


def core_mate():
    z, y, x, core = coords()
    return dev(z, y, x, 1 - core)


def x_mate():
    z, y, x, core = coords()
    return dev(z, y, x + 1 - 2 * lax.rem(x, 2), core)


def z_mate():
    z, y, x, core = coords()
    return dev(z + 1 - 2 * lax.rem(z, 2), y, x, core)


def flip_mate():
    z, y, x, core = coords()
    return dev(z, y, 3 - x, core)


def diagonal():
    z, y, x, core = coords()
    return dev(z, y, 3 - x, 1 - core)


def y_peer(step):
    z, y, x, core = coords()
    return dev(z, lax.rem(y + step, 4), x, core)


def enter():
    barrier = pltpu.get_barrier_semaphore()

    def greet(device):
        pl.semaphore_signal(barrier, inc=1, device_id=device, device_id_type=MESH)

    greet(core_mate())
    greet(x_mate())
    greet(z_mate())
    greet(flip_mate())
    greet(diagonal())
    greet(y_peer(1))
    greet(y_peer(3))

    def far(k):
        greet(dest(k))
        greet(source(k))

    each(0, MSGS, far)
    pl.semaphore_wait(barrier, 7 + 2 * MSGS)


def remote(src, dst, send, recv, device):
    return pltpu.make_async_remote_copy(
        src_ref=src, dst_ref=dst, send_sem=send, recv_sem=recv, device_id=device, device_id_type=MESH
    )


def each(lower, upper, body):
    def step(k, carry):
        body(k)
        return carry

    lax.fori_loop(lower, upper, step, 0)


class Dispatch:
    def __init__(self, src, out, send, recv):
        self.src, self.out = src, out
        self.send, self.recv = send, recv

    def hop(self, stage, src, block, k, device):
        return remote(
            src, self.out.at[block, k], self.send.at[stage, k], self.recv.at[stage, k], device
        )

    def first(self, k):
        return self.hop(0, self.src.at[k], 0, k, dest(k))

    def to_core(self, k):
        return self.hop(1, self.out.at[0, k], 1, k, core_mate())

    def to_x(self, k):
        return self.hop(2, self.out.at[0, k], 2, k, x_mate())

    def onward(self, k):
        return self.hop(3, self.out.at[2, k], 3, k, core_mate())

    def start(self):
        each(0, MSGS, lambda k: self.first(k).start())

    def arrive(self, k):
        self.first(k).wait_recv()
        self.to_core(k).start()
        self.to_x(k).start()

    def pass_on(self, k):
        self.to_x(k).wait_recv()
        self.onward(k).start()

    def step(self, k):
        self.arrive(k)
        self.pass_on(k - LAG)

    def spread(self, lower, upper):
        for k in range(lower, min(upper, LAG)):
            self.arrive(k)
        each(max(lower, LAG), upper, self.step)

    def spread_last(self):
        each(MSGS - LAG, MSGS, self.pass_on)

    def finish(self):
        def step(k):
            self.to_core(k).wait_recv()
            self.onward(k).wait_recv()
            self.to_core(k).wait_send()
            self.to_x(k).wait_send()
            self.onward(k).wait_send()

            self.first(k).wait_send()

        each(0, MSGS, step)


class Ring:
    def __init__(self, src, own, left, right, far, send, recv):
        self.up = remote(src, left, send.at[0], recv.at[0], y_peer(1))
        self.down = remote(src, right, send.at[1], recv.at[1], y_peer(3))
        self.up2 = remote(own(1, 0), far(0), send.at[2], recv.at[2], y_peer(1))
        self.down2 = remote(own(2, 1), far(1), send.at[3], recv.at[3], y_peer(3))

    def start(self):
        self.up.start()
        self.down.start()

    def middle(self):
        self.up.wait_recv()
        self.up2.start()
        self.down.wait_recv()
        self.down2.start()

    def finish(self):
        self.up2.wait_recv()
        self.down2.wait_recv()

    def drain(self):
        for copy in (self.up, self.down, self.up2, self.down2):
            copy.wait_send()


class Quad:
    def __init__(self, src, buf, send, recv):
        n = src.shape[0]
        self.mate = remote(src, buf.at[pl.ds(n, n)], send.at[0], recv.at[0], core_mate())
        self.flip = remote(src, buf.at[pl.ds(2 * n, n)], send.at[1], recv.at[1], flip_mate())
        self.far = remote(
            buf.at[pl.ds(2 * n, n)], buf.at[pl.ds(3 * n, n)], send.at[2], recv.at[2], core_mate()
        )

    def start(self):
        self.flip.start()
        self.mate.start()

    def middle(self):
        self.flip.wait_recv()
        self.far.start()

    def finish(self):
        self.mate.wait_recv()
        self.far.wait_recv()

    def drain(self):
        for copy in (self.mate, self.flip, self.far):
            copy.wait_send()


def kv_ring(buf, base, send, recv):
    return Ring(
        buf.at[base],
        lambda block, h: buf.at[base + block, h],
        buf.at[base + 1],
        buf.at[base + 2],
        lambda h: buf.at[base + 3, h],
        send,
        recv,
    )


def place(chooser, tokens, scale, placed):
    width = 512

    def step(j):
        cols = pl.ds(pl.multiple_of(j * width, width), width)
        rows = jnp.dot(chooser[...], tokens[:, cols], preferred_element_type=F32)
        if scale is not None:
            rows = rows * scale[...]
        for k in range(MSGS):
            placed[k, :, cols] = rows[k * ROWS : (k + 1) * ROWS].astype(BF)

    each(0, tokens.shape[1] // width, step)


def attend(queries, kvall, attended, h):
    cols = pl.ds(pl.multiple_of(h * HD, HD), HD)
    keys = kvall[:, 0, :, cols].reshape(-1, HD)
    values = kvall[:, 1, :, cols].reshape(-1, HD)
    scores = lax.dot_general(
        queries[:, cols], keys, (((1,), (1,)), ((), ())), preferred_element_type=F32
    ) * HD ** (-0.5)
    exponent = jnp.exp(scores - jnp.max(scores, axis=1, keepdims=True))
    total = jnp.sum(exponent, axis=1, keepdims=True)
    mixed = jnp.dot(exponent.astype(BF), values, preferred_element_type=F32)
    attended[:, cols] = (mixed / total).astype(BF)


def forward_kernel(
    keys, values, out_proj, og, queries, tokens, mod_scale, mod_shift, small, want,
    cot, expert_in, mixed, hi, lo,
    kvall, ogall, nall, smallall, ready, scale, placed_cot, placed_in, chooser, attended, normed, proj,
    load, kv_s, kv_r, og_s, og_r, small_s, small_r, n_s, n_r, c_s, c_r, d_s, d_r,
):
    n, width = og.shape
    key_load = pltpu.make_async_copy(keys, kvall.at[0, 0], load.at[0])
    value_load = pltpu.make_async_copy(values, kvall.at[0, 1], load.at[1])
    proj_load = pltpu.make_async_copy(out_proj, proj, load.at[2])
    key_load.start()
    value_load.start()
    proj_load.start()
    names = lax.broadcasted_iota(jnp.int32, (64, n), 0).astype(F32)
    hit0 = names == small[0:1, :]
    hit1 = names == small[1:2, :]
    earlier = lax.broadcasted_iota(jnp.int32, (n, n), 0) < lax.broadcasted_iota(jnp.int32, (n, n), 1)
    named = jnp.where(hit0, 1.0, 0.0) + jnp.where(hit1, 1.0, 0.0)
    before = jnp.dot(named.astype(BF), jnp.where(earlier, 1.0, 0.0).astype(BF), preferred_element_type=F32)
    slot0 = jnp.sum(jnp.where(hit0, before, 0.0), axis=0, keepdims=True)
    slot1 = jnp.sum(jnp.where(hit1, before, 0.0), axis=0, keepdims=True)
    ready[0:1, :] = small[0:1, :] * CAP + slot0
    ready[1:2, :] = small[1:2, :] * CAP + slot1
    ready[2:8, :] = small[2:8, :]
    enter()
    small_sends = [
        remote(ready, smallall.at[s], small_s.at[s - 1], small_r.at[s - 1], device)
        for s, device in ((1, core_mate()), (2, flip_mate()), (3, diagonal()))
    ]
    for copy in small_sends:
        copy.start()
    og_quad = Quad(og, ogall, og_s, og_r)
    og_quad.start()
    key_load.wait()
    value_load.wait()
    zed = remote(kvall.at[0], kvall.at[4], kv_s.at[0, 4], kv_r.at[0, 4], z_mate())
    zed.start()
    near = kv_ring(kvall, 0, kv_s.at[0], kv_r.at[0])
    near.start()
    ogall[0:n] = og[...]
    smallall[0] = ready[...]
    for copy in small_sends:
        copy.wait_recv()
    total = jnp.zeros((MSGS * ROWS, 1), F32)
    for block in range(4):
        shift = float(block * 64 * CAP)
        hit0 = want[...] == smallall[block, 0:1, :] + shift
        hit1 = want[...] == smallall[block, 1:2, :] + shift
        gate = jnp.where(hit0, smallall[block, 2:3, :], 0.0) + jnp.where(hit1, smallall[block, 3:4, :], 0.0)
        picks = jnp.where(hit0, 1.0, 0.0) + jnp.where(hit1, 1.0, 0.0)
        chooser[:, block * n : (block + 1) * n] = picks.astype(BF)
        turned = gate.T
        top = turned.astype(BF)
        hi[block * n : (block + 1) * n, :] = top
        lo[block * n : (block + 1) * n, :] = (turned - top.astype(F32)).astype(BF)
        total = total + jnp.sum(gate, axis=1, keepdims=True)
    scale[...] = total
    og_quad.middle()
    zed.wait_recv()
    other = kv_ring(kvall, 4, kv_s.at[1], kv_r.at[1])
    other.start()
    near.middle()
    og_quad.finish()
    place(chooser, ogall, scale, placed_cot)
    cot_sends = Dispatch(placed_cot, cot, c_s, c_r)
    cot_sends.start()
    cot_sends.spread(0, 2)
    other.middle()
    cot_sends.spread(2, 5)
    near.finish()
    other.finish()

    def attend_and_spread(h):
        attend(queries, kvall, attended, h)
        cot_sends.step(h + 5)

    each(0, HEADS, attend_and_spread)
    proj_load.wait()
    part = 512
    squares = jnp.zeros((n, 1), F32)
    for j in range(width // part):
        cols = slice(j * part, (j + 1) * part)
        value = tokens[:, cols].astype(F32) + jnp.dot(
            attended[...], proj[:, cols], preferred_element_type=F32
        )
        mixed[:, cols] = value
        squares = squares + jnp.sum(value * value, axis=1, keepdims=True)
    inverse = lax.rsqrt(squares * (1.0 / width) + 1e-06)
    normed[...] = (mixed[...] * inverse * (1.0 + mod_scale[...]) + mod_shift[...]).astype(BF)
    quad = Quad(normed, nall, n_s, n_r)
    quad.start()
    nall[0:n] = normed[...]
    cot_sends.spread(13, 16)
    cot_sends.spread_last()
    quad.middle()
    quad.finish()
    place(chooser, nall, None, placed_in)
    sends = Dispatch(placed_in, expert_in, d_s, d_r)
    sends.start()
    sends.spread(0, MSGS)
    sends.spread_last()
    cot_sends.finish()
    sends.finish()
    quad.drain()
    og_quad.drain()
    near.drain()
    other.drain()
    zed.wait_send()
    for copy in small_sends:
        copy.wait_send()


PARTS = 2


def expert_kernel(
    rows_in, cots_in, w_gate, w_up, w_down, hi, lo,
    out, grad_gate, grad_up, grad_down,
    rows, cots, gate, up, hidden_t, gate_t, up_t,
    pieces, from_core, from_diag, pair, from_x, summed, back, flat, middle, partial, peers,
    load, c_s, c_r, b_s, b_r, p_s, p_r,
):
    block_rows = MSGS * ROWS
    n, width = out.shape
    size = width // PARTS
    part = 512
    order = (3, 1, 2, 0)

    def window(block):
        return pl.ds(block * block_rows, block_rows)

    row_loads = [
        pltpu.make_async_copy(rows_in.at[window(block)], rows.at[window(block)], load.at[block])
        for block in order
    ]
    cot_load = pltpu.make_async_copy(cots_in, cots, load.at[4])
    for copy in row_loads:
        copy.start()
    cot_load.start()
    enter()

    def mate_own(c, k):
        return remote(pieces.at[c, 1, k], from_core.at[c, k], c_s.at[c, 0, k], c_r.at[c, 0, k], core_mate())

    def mate_diag(c, k):
        return remote(pieces.at[c, 3, k], from_diag.at[c, k], c_s.at[c, 1, k], c_r.at[c, 1, k], core_mate())

    def across(c, k):
        return remote(pair.at[c, k], from_x.at[c, k], c_s.at[c, 2, k], c_r.at[c, 2, k], x_mate())

    def home(c, k):
        return remote(summed.at[c, k], back.at[c, k], b_s.at[c, k], b_r.at[c, k], source(k))

    across_dims = (((1,), (1,)), ((), ()))
    for block, copy in zip(order, row_loads):
        copy.wait()
        mine = window(block)
        g = lax.dot_general(rows[mine, :], w_gate[...], across_dims, preferred_element_type=F32)
        u = lax.dot_general(rows[mine, :], w_up[...], across_dims, preferred_element_type=F32)
        gate[mine, :] = g
        up[mine, :] = u
        h = g * jax.nn.sigmoid(g) * u
        hidden = h.astype(BF)
        hidden_t[:, block * block_rows : (block + 1) * block_rows] = h.T.astype(BF)
        for j in range(width // part):
            value = jnp.dot(hidden, w_down[:, j * part : (j + 1) * part], preferred_element_type=F32)
            c, base = j * part // size, j * part % size
            for k in range(MSGS):
                pieces[c, block, k, :, base : base + part] = value[k * ROWS : (k + 1) * ROWS].astype(BF)
        if block == 3:
            for c in range(PARTS):
                each(0, MSGS, lambda k: mate_diag(c, k).start())
        if block == 1:
            for c in range(PARTS):
                each(0, MSGS, lambda k: mate_own(c, k).start())

    for c in range(PARTS):

        def add_pair(k):
            mate_diag(c, k).wait_recv()
            pair[c, k] = (pieces[c, 2, k].astype(F32) + from_diag[c, k].astype(F32)).astype(BF)
            across(c, k).start()

        each(0, MSGS, add_pair)

    cot_load.wait()
    for block in range(4):
        mine = window(block)
        hidden_grad = lax.dot_general(cots[mine, :], w_down[...], across_dims, preferred_element_type=F32)
        g = gate[mine, :]
        sg = jax.nn.sigmoid(g)
        columns = slice(block * block_rows, (block + 1) * block_rows)
        gate_t[:, columns] = (hidden_grad * up[mine, :] * sg * (1.0 + g * (1.0 - sg))).T.astype(BF)
        up_t[:, columns] = (hidden_grad * (g * sg)).T.astype(BF)

    for c in range(PARTS):
        cols = slice(c * size, (c + 1) * size)

        def total(k):
            mate_own(c, k).wait_recv()
            across(c, k).wait_recv()
            value = pieces[c, 0, k].astype(F32) + from_core[c, k].astype(F32) + from_x[c, k].astype(F32)
            return value.astype(BF)

        def send_home(k):
            summed[c, k] = total(k)
            home(c, k).start()

        each(0, MSGS, send_home)

    def gradients(j):
        cols = pl.ds(pl.multiple_of(j * part, part), part)
        grad_down[:, cols] = jnp.dot(hidden_t[...], cots[:, cols], preferred_element_type=F32).astype(BF)
        grad_gate[:, cols] = jnp.dot(gate_t[...], rows[:, cols], preferred_element_type=F32).astype(BF)
        grad_up[:, cols] = jnp.dot(up_t[...], rows[:, cols], preferred_element_type=F32).astype(BF)

    each(0, width // part, gradients)

    def to_peer(c, block):
        b = block - 1
        device = flip_mate() if block == 2 else core_mate()
        return remote(partial.at[c, b], peers.at[c, b], p_s.at[c, b], p_r.at[c, b], device)

    for c in range(PARTS):
        cols = slice(c * size, (c + 1) * size)

        def take(k):
            home(c, k).wait_recv()
            flat[pl.ds(pl.multiple_of(k * ROWS, 8), ROWS), cols] = back[c, k].astype(F32)

        each(0, MSGS, take)
        for block in (3, 2, 1, 0):
            mine = slice(block * n, (block + 1) * n)
            for j in range(size // part):
                at = c * size + j * part
                values = flat[:, at : at + part].astype(BF)
                value = jnp.dot(hi[mine], values, preferred_element_type=F32) + jnp.dot(
                    lo[mine], values, preferred_element_type=F32
                )
                here = slice(j * part, (j + 1) * part)
                if block == 2:
                    middle[c, :, here] = value
                elif block:
                    partial[c, block - 1, :, here] = value.astype(BF)
                else:
                    out[:, at : at + part] = value
            if block == 3 or block == 1:
                to_peer(c, block).start()
            if block == 1:
                to_peer(c, 3).wait_recv()
                partial[c, 1] = (middle[c] + peers[c, 2].astype(F32)).astype(BF)
                to_peer(c, 2).start()
    for c in range(PARTS):
        cols = slice(c * size, (c + 1) * size)
        for block in (1, 2):
            to_peer(c, block).wait_recv()
            out[:, cols] += peers[c, block - 1].astype(F32)
    for c in range(PARTS):
        for block in (1, 2, 3):
            to_peer(c, block).wait_send()

        def drain(k):
            mate_diag(c, k).wait_send()
            mate_own(c, k).wait_send()
            across(c, k).wait_send()
            home(c, k).wait_send()

        each(0, MSGS, drain)


def finish_kernel(mixed, combined, a, b, c, out, a_out, b_out, c_out):
    out[...] = (mixed[...] + combined[...]).astype(BF)
    a_out[...] = a[...]
    b_out[...] = b[...]
    c_out[...] = c[...]


def call(kernel, number, outs, scratch, args, in_specs=None, out_specs=None):
    return pl.pallas_call(
        kernel,
        out_shape=outs,
        in_specs=in_specs or [VMEM] * len(args),
        out_specs=out_specs or jax.tree.map(lambda _: VMEM, outs),
        scratch_shapes=scratch,
        compiler_params=pltpu.CompilerParams(
            collective_id=number, has_side_effects=True, vmem_limit_bytes=67043328
        ),
    )(*args)


def per_device(
    tokens,
    queries,
    keys,
    values,
    out_proj,
    mod_scale,
    mod_shift,
    expert_ids,
    gates,
    w_gate,
    w_up,
    w_down,
    out_grad,
):
    n = tokens.shape[1]
    width = tokens.shape[2]
    inner = queries.shape[2]
    rows = MSGS * ROWS
    z, y, x, core = coords()
    small = jnp.concatenate(
        [expert_ids[0].T.astype(F32), gates[0].T, jnp.zeros((4, n), F32)], axis=0
    )
    row = jnp.arange(rows, dtype=jnp.int32)
    dz, dy = offset(row // ROWS, core)
    to_z = (z + dz) % 8
    expert = ((to_z % 2) * 4 + (y + dy) % 4) * 8 + (to_z // 2) * 2 + x // 2
    want = (row % ROWS // CAP) * (64 * CAP) + expert * CAP + row % CAP
    want = jnp.broadcast_to(want.astype(F32)[:, None], (rows, n))

    slots = jax.ShapeDtypeStruct((4, MSGS, ROWS, width), BF)
    routed = jax.ShapeDtypeStruct((YN * n, rows), BF)
    cot, expert_in, mixed, hi, lo = call(
        forward_kernel,
        1,
        (slots, slots, jax.ShapeDtypeStruct((n, width), F32), routed, routed),
        [
            pltpu.VMEM((8, 2, n, inner), BF),
            pltpu.VMEM((YN * n, width), BF),
            pltpu.VMEM((YN * n, width), BF),
            pltpu.VMEM((YN, 8, n), F32),
            pltpu.VMEM((8, n), F32),
            pltpu.VMEM((rows, 1), F32),
            pltpu.VMEM((MSGS, ROWS, width), BF),
            pltpu.VMEM((MSGS, ROWS, width), BF),
            pltpu.VMEM((rows, YN * n), BF),
            pltpu.VMEM((n, inner), BF),
            pltpu.VMEM((n, width), BF),
            pltpu.VMEM((inner, width), BF),
            DMA((3,)),
            DMA((2, 5)),
            DMA((2, 5)),
            DMA((3,)),
            DMA((3,)),
            DMA((3,)),
            DMA((3,)),
            DMA((3,)),
            DMA((3,)),
            DMA((4, MSGS)),
            DMA((4, MSGS)),
            DMA((4, MSGS)),
            DMA((4, MSGS)),
        ],
        (keys[0], values[0], out_proj, out_grad[0], queries[0], tokens[0], mod_scale, mod_shift, small, want),
        in_specs=[ANY] * 3 + [VMEM] * 7,
        out_specs=(ANY, ANY, VMEM, VMEM, VMEM),
    )
    everything = 4 * rows
    hid = w_gate.shape[0]
    block = pltpu.VMEM((PARTS, MSGS, ROWS, width // PARTS), BF)
    share = pltpu.VMEM((PARTS, 3, n, width // PARTS), BF)
    grad = jax.ShapeDtypeStruct((hid, width), BF)
    combined, grad_gate, grad_up, grad_down = call(
        expert_kernel,
        2,
        (jax.ShapeDtypeStruct((n, width), F32), grad, grad, grad),
        [
            pltpu.VMEM((everything, width), BF),
            pltpu.VMEM((everything, width), BF),
            pltpu.VMEM((everything, hid), F32),
            pltpu.VMEM((everything, hid), F32),
            pltpu.VMEM((hid, everything), BF),
            pltpu.VMEM((hid, everything), BF),
            pltpu.VMEM((hid, everything), BF),
            pltpu.VMEM((PARTS, 4, MSGS, ROWS, width // PARTS), BF),
            block,
            block,
            block,
            block,
            block,
            block,
            pltpu.VMEM((rows, width), F32),
            pltpu.VMEM((PARTS, n, width // PARTS), F32),
            share,
            share,
            DMA((5,)),
            DMA((PARTS, 3, MSGS)),
            DMA((PARTS, 3, MSGS)),
            DMA((PARTS, MSGS)),
            DMA((PARTS, MSGS)),
            DMA((PARTS, 3)),
            DMA((PARTS, 3)),
        ],
        (expert_in.reshape(everything, width), cot.reshape(everything, width), w_gate, w_up, w_down, hi, lo),
        in_specs=[ANY] * 2 + [VMEM] * 5,
    )
    steps = 4
    thin = pl.BlockSpec((n // steps, width), lambda i: (i, 0))
    thick = pl.BlockSpec((hid // steps, width), lambda i: (i, 0))
    layer_out, grad_gate, grad_up, grad_down = pl.pallas_call(
        finish_kernel,
        grid=(steps,),
        in_specs=[thin, thin, thick, thick, thick],
        out_specs=(thin, thick, thick, thick),
        out_shape=(jax.ShapeDtypeStruct((n, width), BF), grad, grad, grad),
    )(mixed, combined, grad_gate, grad_up, grad_down)
    return (layer_out[None], grad_gate, grad_up, grad_down)


def solution(mesh):
    placed = (
        P("exp", "ctx", None),
        P("exp", "ctx", None),
        P("exp", "ctx", None),
        P("exp", "ctx", None),
        P(),
        P("exp", None),
        P("exp", None),
        P("exp", "ctx", None),
        P("exp", "ctx", None),
        P(("ctx", "exp"), None),
        P(("ctx", "exp"), None),
        P(("ctx", "exp"), None),
        P("exp", "ctx", None),
    )
    return jax.shard_map(
        per_device,
        mesh=mesh,
        in_specs=placed,
        out_specs=(
            P("exp", "ctx", None),
            P(("ctx", "exp"), None),
            P(("ctx", "exp"), None),
            P(("ctx", "exp"), None),
        ),
        check_vma=False,
    )
```

```python
import jax
import jax.numpy as jnp
from jax import lax
from jax.experimental import pallas as pl
from jax.experimental.pallas import tpu as pltpu
from jax.sharding import PartitionSpec as P

HEADS = 8
HD = 128
SHARDS = 4
CAP = 6
YN = 4
MSGS = 16
ROWS = YN * CAP
LAG = 3
MESH = pl.DeviceIdType.MESH
BF = jnp.bfloat16
F32 = jnp.float32
VMEM = pl.BlockSpec(memory_space=pltpu.VMEM)
ANY = pl.BlockSpec(memory_space=pl.ANY)
DMA = pltpu.SemaphoreType.DMA


def coords():
    c = lax.axis_index("ctx")
    e = lax.axis_index("exp")
    z = lax.div(e, 8) * 2 + lax.div(c, 4)
    return z, lax.rem(c, 4), lax.rem(lax.div(e, 2), 4), lax.rem(e, 2)


def dev(z, y, x, core):
    return {"ctx": lax.rem(z, 2) * 4 + y, "exp": lax.div(z, 2) * 8 + x * 2 + core}


def offset(k, core):
    t = lax.rem(k, 4)
    return 2 * (t + lax.div(t, 2) * (1 - 2 * lax.rem(t, 2))) + core, lax.div(k, 4)


def dest(k):
    z, y, x, core = coords()
    dz, dy = offset(k, core)
    return dev(lax.rem(z + dz, 8), lax.rem(y + dy, 4), x, 1 - core)


def source(k):
    z, y, x, core = coords()
    dz, dy = offset(k, 1 - core)
    return dev(lax.rem(z + 8 - dz, 8), lax.rem(y + 4 - dy, 4), x, 1 - core)


def core_mate():
    z, y, x, core = coords()
    return dev(z, y, x, 1 - core)


def x_mate():
    z, y, x, core = coords()
    return dev(z, y, x + 1 - 2 * lax.rem(x, 2), core)


def z_mate():
    z, y, x, core = coords()
    return dev(z + 1 - 2 * lax.rem(z, 2), y, x, core)


def flip_mate():
    z, y, x, core = coords()
    return dev(z, y, 3 - x, core)


def diagonal():
    z, y, x, core = coords()
    return dev(z, y, 3 - x, 1 - core)


def y_peer(step):
    z, y, x, core = coords()
    return dev(z, lax.rem(y + step, 4), x, core)


def hello():
    barrier = pltpu.get_barrier_semaphore()

    def greet(device):
        pl.semaphore_signal(barrier, inc=1, device_id=device, device_id_type=MESH)

    greet(core_mate())
    greet(x_mate())
    greet(z_mate())
    greet(flip_mate())
    greet(diagonal())
    greet(y_peer(1))
    greet(y_peer(3))

    def far(k):
        greet(dest(k))
        greet(source(k))

    each(0, MSGS, far)


def everyone_here():
    pl.semaphore_wait(pltpu.get_barrier_semaphore(), 7 + 2 * MSGS)


def remote(src, dst, send, recv, device):
    return pltpu.make_async_remote_copy(
        src_ref=src, dst_ref=dst, send_sem=send, recv_sem=recv, device_id=device, device_id_type=MESH
    )


def each(lower, upper, body):
    def step(k, carry):
        body(k)
        return carry

    lax.fori_loop(lower, upper, step, 0)


class Dispatch:
    def __init__(self, src, out, send, recv):
        self.src, self.out = src, out
        self.send, self.recv = send, recv

    def hop(self, stage, src, block, k, device):
        return remote(
            src, self.out.at[block, k], self.send.at[stage, k], self.recv.at[stage, k], device
        )

    def first(self, k):
        return self.hop(0, self.src.at[k], 0, k, dest(k))

    def to_core(self, k):
        return self.hop(1, self.out.at[0, k], 1, k, core_mate())

    def to_x(self, k):
        return self.hop(2, self.out.at[0, k], 2, k, x_mate())

    def onward(self, k):
        return self.hop(3, self.out.at[2, k], 3, k, core_mate())

    def start(self):
        each(0, MSGS, lambda k: self.first(k).start())

    def arrive(self, k):
        self.first(k).wait_recv()
        self.to_core(k).start()
        self.to_x(k).start()

    def pass_on(self, k):
        self.to_x(k).wait_recv()
        self.onward(k).start()

    def step(self, k):
        self.arrive(k)
        self.pass_on(k - LAG)

    def spread(self, lower, upper):
        for k in range(lower, min(upper, LAG)):
            self.arrive(k)
        each(max(lower, LAG), upper, self.step)

    def spread_last(self):
        each(MSGS - LAG, MSGS, self.pass_on)

    def finish(self):
        def step(k):
            self.to_core(k).wait_recv()
            self.onward(k).wait_recv()
            self.to_core(k).wait_send()
            self.to_x(k).wait_send()
            self.onward(k).wait_send()

            self.first(k).wait_send()

        each(0, MSGS, step)


class Ring:
    def __init__(self, src, own, left, right, far, send, recv):
        self.up = remote(src, left, send.at[0], recv.at[0], y_peer(1))
        self.down = remote(src, right, send.at[1], recv.at[1], y_peer(3))
        self.up2 = remote(own(1, 0), far(0), send.at[2], recv.at[2], y_peer(1))
        self.down2 = remote(own(2, 1), far(1), send.at[3], recv.at[3], y_peer(3))

    def start(self):
        self.up.start()
        self.down.start()

    def middle(self):
        self.up.wait_recv()
        self.up2.start()
        self.down.wait_recv()
        self.down2.start()

    def finish(self):
        self.up2.wait_recv()
        self.down2.wait_recv()

    def drain(self):
        for copy in (self.up, self.down, self.up2, self.down2):
            copy.wait_send()


class Quad:
    def __init__(self, src, buf, send, recv):
        n = src.shape[0]
        self.mate = remote(src, buf.at[pl.ds(n, n)], send.at[0], recv.at[0], core_mate())
        self.flip = remote(src, buf.at[pl.ds(2 * n, n)], send.at[1], recv.at[1], flip_mate())
        self.far = remote(
            buf.at[pl.ds(2 * n, n)], buf.at[pl.ds(3 * n, n)], send.at[2], recv.at[2], core_mate()
        )

    def start(self):
        self.flip.start()
        self.mate.start()

    def middle(self):
        self.flip.wait_recv()
        self.far.start()

    def finish(self):
        self.mate.wait_recv()
        self.far.wait_recv()

    def drain(self):
        for copy in (self.mate, self.flip, self.far):
            copy.wait_send()


def kv_ring(buf, base, send, recv):
    return Ring(
        buf.at[base],
        lambda block, h: buf.at[base + block, h],
        buf.at[base + 1],
        buf.at[base + 2],
        lambda h: buf.at[base + 3, h],
        send,
        recv,
    )


def place(chooser, tokens, scale, placed):
    width = 512

    def step(j):
        cols = pl.ds(pl.multiple_of(j * width, width), width)
        rows = jnp.dot(chooser[...], tokens[:, cols], preferred_element_type=F32)
        if scale is not None:
            rows = rows * scale[...]
        for k in range(MSGS):
            placed[k, :, cols] = rows[k * ROWS : (k + 1) * ROWS].astype(BF)

    each(0, tokens.shape[1] // width, step)


def attend(queries, kvall, attended, h):
    cols = pl.ds(pl.multiple_of(h * HD, HD), HD)
    keys = kvall[:, 0, :, cols].reshape(-1, HD)
    values = kvall[:, 1, :, cols].reshape(-1, HD)
    scores = lax.dot_general(
        queries[:, cols], keys, (((1,), (1,)), ((), ())), preferred_element_type=F32
    ) * HD ** (-0.5)
    exponent = jnp.exp(scores - jnp.max(scores, axis=1, keepdims=True))
    total = jnp.sum(exponent, axis=1, keepdims=True)
    mixed = jnp.dot(exponent.astype(BF), values, preferred_element_type=F32)
    attended[:, cols] = (mixed / total).astype(BF)


def forward_kernel(
    keys, values, out_proj, og, queries, tokens, mod_scale, mod_shift, small, want,
    cot, expert_in, mixed, hi, lo,
    kvall, ogall, nall, smallall, ready, scale, placed_cot, placed_in, chooser, attended, normed, proj,
    load, kv_s, kv_r, og_s, og_r, small_s, small_r, n_s, n_r, c_s, c_r, d_s, d_r,
):
    n, width = og.shape
    hello()
    key_load = pltpu.make_async_copy(keys, kvall.at[0, 0], load.at[0])
    value_load = pltpu.make_async_copy(values, kvall.at[0, 1], load.at[1])
    proj_load = pltpu.make_async_copy(out_proj, proj, load.at[2])
    key_load.start()
    value_load.start()
    proj_load.start()
    names = lax.broadcasted_iota(jnp.int32, (64, n), 0).astype(F32)
    hit0 = names == small[0:1, :]
    hit1 = names == small[1:2, :]
    earlier = lax.broadcasted_iota(jnp.int32, (n, n), 0) < lax.broadcasted_iota(jnp.int32, (n, n), 1)
    named = jnp.where(hit0, 1.0, 0.0) + jnp.where(hit1, 1.0, 0.0)
    before = jnp.dot(named.astype(BF), jnp.where(earlier, 1.0, 0.0).astype(BF), preferred_element_type=F32)
    slot0 = jnp.sum(jnp.where(hit0, before, 0.0), axis=0, keepdims=True)
    slot1 = jnp.sum(jnp.where(hit1, before, 0.0), axis=0, keepdims=True)
    ready[0:1, :] = small[0:1, :] * CAP + slot0
    ready[1:2, :] = small[1:2, :] * CAP + slot1
    ready[2:8, :] = small[2:8, :]
    everyone_here()
    small_sends = [
        remote(ready, smallall.at[s], small_s.at[s - 1], small_r.at[s - 1], device)
        for s, device in ((1, core_mate()), (2, flip_mate()), (3, diagonal()))
    ]
    for copy in small_sends:
        copy.start()
    og_quad = Quad(og, ogall, og_s, og_r)
    og_quad.start()
    key_load.wait()
    value_load.wait()
    zed = remote(kvall.at[0], kvall.at[4], kv_s.at[0, 4], kv_r.at[0, 4], z_mate())
    zed.start()
    near = kv_ring(kvall, 0, kv_s.at[0], kv_r.at[0])
    near.start()
    ogall[0:n] = og[...]
    smallall[0] = ready[...]
    for copy in small_sends:
        copy.wait_recv()
    total = jnp.zeros((MSGS * ROWS, 1), F32)
    for block in range(4):
        shift = float(block * 64 * CAP)
        hit0 = want[...] == smallall[block, 0:1, :] + shift
        hit1 = want[...] == smallall[block, 1:2, :] + shift
        gate = jnp.where(hit0, smallall[block, 2:3, :], 0.0) + jnp.where(hit1, smallall[block, 3:4, :], 0.0)
        picks = jnp.where(hit0, 1.0, 0.0) + jnp.where(hit1, 1.0, 0.0)
        chooser[:, block * n : (block + 1) * n] = picks.astype(BF)
        turned = gate.T
        top = turned.astype(BF)
        hi[block * n : (block + 1) * n, :] = top
        lo[block * n : (block + 1) * n, :] = (turned - top.astype(F32)).astype(BF)
        total = total + jnp.sum(gate, axis=1, keepdims=True)
    scale[...] = total
    og_quad.middle()
    zed.wait_recv()
    other = kv_ring(kvall, 4, kv_s.at[1], kv_r.at[1])
    other.start()
    near.middle()
    og_quad.finish()
    place(chooser, ogall, scale, placed_cot)
    cot_sends = Dispatch(placed_cot, cot, c_s, c_r)
    cot_sends.start()
    cot_sends.spread(0, 2)
    other.middle()
    cot_sends.spread(2, 5)
    near.finish()
    other.finish()

    def attend_and_spread(h):
        attend(queries, kvall, attended, h)
        cot_sends.step(h + 5)

    each(0, HEADS, attend_and_spread)
    proj_load.wait()
    part = 512
    squares = jnp.zeros((n, 1), F32)
    for j in range(width // part):
        cols = slice(j * part, (j + 1) * part)
        value = tokens[:, cols].astype(F32) + jnp.dot(
            attended[...], proj[:, cols], preferred_element_type=F32
        )
        mixed[:, cols] = value
        squares = squares + jnp.sum(value * value, axis=1, keepdims=True)
    inverse = lax.rsqrt(squares * (1.0 / width) + 1e-06)
    normed[...] = (mixed[...] * inverse * (1.0 + mod_scale[...]) + mod_shift[...]).astype(BF)
    quad = Quad(normed, nall, n_s, n_r)
    quad.start()
    nall[0:n] = normed[...]
    cot_sends.spread(13, 16)
    cot_sends.spread_last()
    quad.middle()
    quad.finish()
    place(chooser, nall, None, placed_in)
    sends = Dispatch(placed_in, expert_in, d_s, d_r)
    sends.start()
    sends.spread(0, MSGS)
    sends.spread_last()
    cot_sends.finish()
    sends.finish()
    quad.drain()
    og_quad.drain()
    near.drain()
    other.drain()
    zed.wait_send()
    for copy in small_sends:
        copy.wait_send()


PARTS = 2


def expert_kernel(
    rows_in, cots_in, w_gate, w_up, w_down, hi, lo,
    out, grad_gate, grad_up, grad_down,
    rows, cots, gate, up, hidden_t, gate_t, up_t,
    pieces, from_core, from_diag, pair, from_x, summed, back, flat, middle, partial, peers,
    load, c_s, c_r, b_s, b_r, p_s, p_r,
):
    block_rows = MSGS * ROWS
    n, width = out.shape
    size = width // PARTS
    part = 512
    order = (3, 1, 2, 0)

    def window(block):
        return pl.ds(block * block_rows, block_rows)

    row_loads = [
        pltpu.make_async_copy(rows_in.at[window(block)], rows.at[window(block)], load.at[block])
        for block in order
    ]
    cot_load = pltpu.make_async_copy(cots_in, cots, load.at[4])
    for copy in row_loads:
        copy.start()
    cot_load.start()
    hello()

    def mate_own(c, k):
        return remote(pieces.at[c, 1, k], from_core.at[c, k], c_s.at[c, 0, k], c_r.at[c, 0, k], core_mate())

    def mate_diag(c, k):
        return remote(pieces.at[c, 3, k], from_diag.at[c, k], c_s.at[c, 1, k], c_r.at[c, 1, k], core_mate())

    def across(c, k):
        return remote(pair.at[c, k], from_x.at[c, k], c_s.at[c, 2, k], c_r.at[c, 2, k], x_mate())

    def home(c, k):
        return remote(summed.at[c, k], back.at[c, k], b_s.at[c, k], b_r.at[c, k], source(k))

    across_dims = (((1,), (1,)), ((), ()))
    for block, copy in zip(order, row_loads):
        copy.wait()
        mine = window(block)
        g = lax.dot_general(rows[mine, :], w_gate[...], across_dims, preferred_element_type=F32)
        u = lax.dot_general(rows[mine, :], w_up[...], across_dims, preferred_element_type=F32)
        gate[mine, :] = g
        up[mine, :] = u
        h = g * jax.nn.sigmoid(g) * u
        hidden = h.astype(BF)
        hidden_t[:, block * block_rows : (block + 1) * block_rows] = h.T.astype(BF)
        for j in range(width // part):
            value = jnp.dot(hidden, w_down[:, j * part : (j + 1) * part], preferred_element_type=F32)
            c, base = j * part // size, j * part % size
            for k in range(MSGS):
                pieces[c, block, k, :, base : base + part] = value[k * ROWS : (k + 1) * ROWS].astype(BF)
        if block == 3:
            everyone_here()
            for c in range(PARTS):
                each(0, MSGS, lambda k: mate_diag(c, k).start())
        if block == 1:
            for c in range(PARTS):
                each(0, MSGS, lambda k: mate_own(c, k).start())

    for c in range(PARTS):

        def add_pair(k):
            mate_diag(c, k).wait_recv()
            pair[c, k] = (pieces[c, 2, k].astype(F32) + from_diag[c, k].astype(F32)).astype(BF)
            across(c, k).start()

        each(0, MSGS, add_pair)

    cot_load.wait()
    for block in range(4):
        mine = window(block)
        hidden_grad = lax.dot_general(cots[mine, :], w_down[...], across_dims, preferred_element_type=F32)
        g = gate[mine, :]
        sg = jax.nn.sigmoid(g)
        columns = slice(block * block_rows, (block + 1) * block_rows)
        gate_t[:, columns] = (hidden_grad * up[mine, :] * sg * (1.0 + g * (1.0 - sg))).T.astype(BF)
        up_t[:, columns] = (hidden_grad * (g * sg)).T.astype(BF)

    for c in range(PARTS):
        cols = slice(c * size, (c + 1) * size)

        def total(k):
            mate_own(c, k).wait_recv()
            across(c, k).wait_recv()
            value = pieces[c, 0, k].astype(F32) + from_core[c, k].astype(F32) + from_x[c, k].astype(F32)
            return value.astype(BF)

        def send_home(k):
            summed[c, k] = total(k)
            home(c, k).start()

        each(0, MSGS, send_home)

    def gradients(j):
        cols = pl.ds(pl.multiple_of(j * part, part), part)
        grad_down[:, cols] = jnp.dot(hidden_t[...], cots[:, cols], preferred_element_type=F32).astype(BF)
        grad_gate[:, cols] = jnp.dot(gate_t[...], rows[:, cols], preferred_element_type=F32).astype(BF)
        grad_up[:, cols] = jnp.dot(up_t[...], rows[:, cols], preferred_element_type=F32).astype(BF)

    each(0, width // part, gradients)

    def to_peer(c, block):
        b = block - 1
        device = flip_mate() if block == 2 else core_mate()
        return remote(partial.at[c, b], peers.at[c, b], p_s.at[c, b], p_r.at[c, b], device)

    for c in range(PARTS):
        cols = slice(c * size, (c + 1) * size)

        def take(k):
            home(c, k).wait_recv()
            flat[pl.ds(pl.multiple_of(k * ROWS, 8), ROWS), cols] = back[c, k].astype(F32)

        each(0, MSGS, take)
        for block in (3, 2, 1, 0):
            mine = slice(block * n, (block + 1) * n)
            for j in range(size // part):
                at = c * size + j * part
                values = flat[:, at : at + part].astype(BF)
                value = jnp.dot(hi[mine], values, preferred_element_type=F32) + jnp.dot(
                    lo[mine], values, preferred_element_type=F32
                )
                here = slice(j * part, (j + 1) * part)
                if block == 2:
                    middle[c, :, here] = value
                elif block:
                    partial[c, block - 1, :, here] = value.astype(BF)
                else:
                    out[:, at : at + part] = value
            if block == 3 or block == 1:
                to_peer(c, block).start()
            if block == 1:
                to_peer(c, 3).wait_recv()
                partial[c, 1] = (middle[c] + peers[c, 2].astype(F32)).astype(BF)
                to_peer(c, 2).start()
    for c in range(PARTS):
        cols = slice(c * size, (c + 1) * size)
        for block in (1, 2):
            to_peer(c, block).wait_recv()
            out[:, cols] += peers[c, block - 1].astype(F32)
    for c in range(PARTS):
        for block in (1, 2, 3):
            to_peer(c, block).wait_send()

        def drain(k):
            mate_diag(c, k).wait_send()
            mate_own(c, k).wait_send()
            across(c, k).wait_send()
            home(c, k).wait_send()

        each(0, MSGS, drain)


def finish_kernel(mixed, combined, a, b, c, out, a_out, b_out, c_out):
    out[...] = (mixed[...] + combined[...]).astype(BF)
    a_out[...] = a[...]
    b_out[...] = b[...]
    c_out[...] = c[...]


def call(kernel, number, outs, scratch, args, in_specs=None, out_specs=None):
    return pl.pallas_call(
        kernel,
        out_shape=outs,
        in_specs=in_specs or [VMEM] * len(args),
        out_specs=out_specs or jax.tree.map(lambda _: VMEM, outs),
        scratch_shapes=scratch,
        compiler_params=pltpu.CompilerParams(
            collective_id=number, has_side_effects=True, vmem_limit_bytes=67043328
        ),
    )(*args)


def per_device(
    tokens,
    queries,
    keys,
    values,
    out_proj,
    mod_scale,
    mod_shift,
    expert_ids,
    gates,
    w_gate,
    w_up,
    w_down,
    out_grad,
):
    n = tokens.shape[1]
    width = tokens.shape[2]
    inner = queries.shape[2]
    rows = MSGS * ROWS
    z, y, x, core = coords()
    small = jnp.concatenate(
        [expert_ids[0].T.astype(F32), gates[0].T, jnp.zeros((4, n), F32)], axis=0
    )
    row = jnp.arange(rows, dtype=jnp.int32)
    dz, dy = offset(row // ROWS, core)
    to_z = (z + dz) % 8
    expert = ((to_z % 2) * 4 + (y + dy) % 4) * 8 + (to_z // 2) * 2 + x // 2
    want = (row % ROWS // CAP) * (64 * CAP) + expert * CAP + row % CAP
    want = jnp.broadcast_to(want.astype(F32)[:, None], (rows, n))

    slots = jax.ShapeDtypeStruct((4, MSGS, ROWS, width), BF)
    routed = jax.ShapeDtypeStruct((YN * n, rows), BF)
    cot, expert_in, mixed, hi, lo = call(
        forward_kernel,
        1,
        (slots, slots, jax.ShapeDtypeStruct((n, width), F32), routed, routed),
        [
            pltpu.VMEM((8, 2, n, inner), BF),
            pltpu.VMEM((YN * n, width), BF),
            pltpu.VMEM((YN * n, width), BF),
            pltpu.VMEM((YN, 8, n), F32),
            pltpu.VMEM((8, n), F32),
            pltpu.VMEM((rows, 1), F32),
            pltpu.VMEM((MSGS, ROWS, width), BF),
            pltpu.VMEM((MSGS, ROWS, width), BF),
            pltpu.VMEM((rows, YN * n), BF),
            pltpu.VMEM((n, inner), BF),
            pltpu.VMEM((n, width), BF),
            pltpu.VMEM((inner, width), BF),
            DMA((3,)),
            DMA((2, 5)),
            DMA((2, 5)),
            DMA((3,)),
            DMA((3,)),
            DMA((3,)),
            DMA((3,)),
            DMA((3,)),
            DMA((3,)),
            DMA((4, MSGS)),
            DMA((4, MSGS)),
            DMA((4, MSGS)),
            DMA((4, MSGS)),
        ],
        (keys[0], values[0], out_proj, out_grad[0], queries[0], tokens[0], mod_scale, mod_shift, small, want),
        in_specs=[ANY] * 3 + [VMEM] * 7,
        out_specs=(ANY, ANY, VMEM, VMEM, VMEM),
    )
    everything = 4 * rows
    hid = w_gate.shape[0]
    block = pltpu.VMEM((PARTS, MSGS, ROWS, width // PARTS), BF)
    share = pltpu.VMEM((PARTS, 3, n, width // PARTS), BF)
    grad = jax.ShapeDtypeStruct((hid, width), BF)
    combined, grad_gate, grad_up, grad_down = call(
        expert_kernel,
        2,
        (jax.ShapeDtypeStruct((n, width), F32), grad, grad, grad),
        [
            pltpu.VMEM((everything, width), BF),
            pltpu.VMEM((everything, width), BF),
            pltpu.VMEM((everything, hid), F32),
            pltpu.VMEM((everything, hid), F32),
            pltpu.VMEM((hid, everything), BF),
            pltpu.VMEM((hid, everything), BF),
            pltpu.VMEM((hid, everything), BF),
            pltpu.VMEM((PARTS, 4, MSGS, ROWS, width // PARTS), BF),
            block,
            block,
            block,
            block,
            block,
            block,
            pltpu.VMEM((rows, width), F32),
            pltpu.VMEM((PARTS, n, width // PARTS), F32),
            share,
            share,
            DMA((5,)),
            DMA((PARTS, 3, MSGS)),
            DMA((PARTS, 3, MSGS)),
            DMA((PARTS, MSGS)),
            DMA((PARTS, MSGS)),
            DMA((PARTS, 3)),
            DMA((PARTS, 3)),
        ],
        (expert_in.reshape(everything, width), cot.reshape(everything, width), w_gate, w_up, w_down, hi, lo),
        in_specs=[ANY] * 2 + [VMEM] * 5,
    )
    steps = 4
    thin = pl.BlockSpec((n // steps, width), lambda i: (i, 0))
    thick = pl.BlockSpec((hid // steps, width), lambda i: (i, 0))
    layer_out, grad_gate, grad_up, grad_down = pl.pallas_call(
        finish_kernel,
        grid=(steps,),
        in_specs=[thin, thin, thick, thick, thick],
        out_specs=(thin, thick, thick, thick),
        out_shape=(jax.ShapeDtypeStruct((n, width), BF), grad, grad, grad),
    )(mixed, combined, grad_gate, grad_up, grad_down)
    return (layer_out[None], grad_gate, grad_up, grad_down)


def solution(mesh):
    placed = (
        P("exp", "ctx", None),
        P("exp", "ctx", None),
        P("exp", "ctx", None),
        P("exp", "ctx", None),
        P(),
        P("exp", None),
        P("exp", None),
        P("exp", "ctx", None),
        P("exp", "ctx", None),
        P(("ctx", "exp"), None),
        P(("ctx", "exp"), None),
        P(("ctx", "exp"), None),
        P("exp", "ctx", None),
    )
    return jax.shard_map(
        per_device,
        mesh=mesh,
        in_specs=placed,
        out_specs=(
            P("exp", "ctx", None),
            P(("ctx", "exp"), None),
            P(("ctx", "exp"), None),
            P(("ctx", "exp"), None),
        ),
        check_vma=False,
    )
```
